256 devices in a mesh: row: 4 (over x), col: 64 (over y, z, core).
Axes of the slice: x: 4, y: 4, z: 8, core: 2. Of those that a mesh axis runs over, the one named last changes fastest.
Arguments:
- child_rhs: bfloat16 [12288, 128, 128], P(('row', 'col')), may hold values from -6 to 6
- parent_rhs: bfloat16 [64, 128, 128], P('col'), may hold values from -6 to 6
- child_lower_inv: bfloat16 [12288, 128, 128], P(('row', 'col')), may hold values from -0.5 to 0.5
- child_lower_off: bfloat16 [12288, 128, 128], P(('row', 'col')), may hold values from -0.125 to 0.125
- child_upper_inv: bfloat16 [12288, 128, 128], P(('row', 'col')), may hold values from -0.5 to 0.5
- child_upper_off: bfloat16 [12288, 128, 128], P(('row', 'col')), may hold values from -0.25 to 0.25
- parent_lower_inv: bfloat16 [64, 128, 128], P('col'), may hold values from -0.5 to 0.5
- parent_upper_inv: bfloat16 [64, 128, 128], P('col'), may hold values from -0.5 to 0.5
- parent_of: int32 [12288], P(('row', 'col')), may hold values from 0 to 63
Outputs:
- child_solution: bfloat16 [12288, 128, 128], P(('row', 'col'))
- parent_solution: bfloat16 [64, 128, 128], P('col')
The draws below stay inside these ranges and needn't reach their ends.
Inputs may be any that keep to these rules, and one draw needn't show every extreme that they name: `parent_of`: each lower-level supernode names one upper-level parent.
All inputs are finite; a program needn't handle non-finite values.
Results may differ from the reference program's by a relative error of at most 0.0095.
Values may be sent and summed in bfloat16 or wider, within the bound.
A program may use at most 64 MiB of HBM per device.

```python
import math
import jax
import jax.numpy as jnp
import numpy as np
from jax import lax

W = 128
R = 128
CH_DEV = 48
NP = 64
NC = 12288


def touch_ends(array, rng, low, high):
    longest = array.shape.index(max(array.shape))
    spots = []
    for shift in (0, 1):
        where = [jax.random.randint(jax.random.fold_in(rng, axis), (), 0, length) for axis, length in enumerate(array.shape)]
        where[longest] = (where[longest] + shift) % array.shape[longest]
        spots.append(tuple(where))
    return array.at[spots[0]].set(low).at[spots[1]].set(high)


def steps_of(rng, extent, cuts, least, top_value):
    level = 1.0
    for position, parts in cuts:
        steps = jax.random.uniform(jax.random.fold_in(jax.random.fold_in(rng, 6), position), (parts,), jnp.float32, least / len(cuts), top_value / len(cuts))
        level = level * jnp.repeat(jnp.exp(steps), extent[position] // parts).reshape((-1,) + (1,) * (len(extent) - 1 - position))
    return level


def rank_bounds(amount, slope):
    loads = [(1 << 20) // math.isqrt(grade ** slope) + 1 for grade in range(1, amount + 1)]
    scale = 1 + sum(loads) // (1 << 30)
    return np.cumsum(np.array([max(1, weight // scale) for weight in loads]))


def skewed_ids(rng, extent, count, skew):
    table = rank_bounds(count, skew)
    pick = jax.random.randint(jax.random.fold_in(rng, 1), extent, 0, int(table[count - 1]))
    grade = jnp.searchsorted(jnp.asarray(table, jnp.int32), pick, side="right")
    return jax.random.permutation(jax.random.fold_in(rng, 2), count)[grade].astype(jnp.int32)


def centred(key, extent, scale, bound, split=(), kind=jnp.bfloat16):
    factor_of = steps_of(key, extent, split, -0.22, 0.18) if split else 1.0
    result = jax.random.normal(key, extent, jnp.float32) * scale * factor_of
    return jnp.minimum(jnp.maximum(result, -bound), bound).astype(kind)


def setup_inputs(seed: int = 0) -> dict:
    splits = jax.random.split(jax.random.key(seed), 10)
    child_rhs = centred(splits[0], (NC, W, R), 1.0, 6.0, ((0, 256),))
    parent_rhs = centred(splits[1], (NP, W, R), 1.0, 6.0, ((0, 64),))
    child_lower_inv = centred(splits[2], (NC, W, W), W ** -0.5, 0.5, ((0, 256),))
    child_lower_off = centred(splits[3], (NC, W, W), (W * 16) ** -0.5, 0.125, ((0, 256),))
    child_upper_inv = centred(splits[4], (NC, W, W), W ** -0.5, 0.5, ((0, 256),))
    child_upper_off = centred(splits[5], (NC, W, W), (W * 4) ** -0.5, 0.25, ((0, 256),))
    parent_lower_inv = centred(splits[6], (NP, W, W), W ** -0.5, 0.5, ((0, 64),))
    parent_upper_inv = centred(splits[7], (NP, W, W), W ** -0.5, 0.5, ((0, 64),))
    parent_of = touch_ends(skewed_ids(splits[8], (NC,), NP, 1), jax.random.fold_in(splits[8], 3), 0, NP - 1).astype(jnp.int32)
    return {"child_rhs": child_rhs, "parent_rhs": parent_rhs, "child_lower_inv": child_lower_inv, "child_lower_off": child_lower_off, "child_upper_inv": child_upper_inv, "child_upper_off": child_upper_off, "parent_lower_inv": parent_lower_inv, "parent_upper_inv": parent_upper_inv, "parent_of": parent_of}


def bmm(a, b):
    return jnp.einsum('cij,cjr->cir', a.astype(jnp.float32), b.astype(jnp.float32))


def reference(child_rhs, parent_rhs, child_lower_inv, child_lower_off, child_upper_inv, child_upper_off, parent_lower_inv, parent_upper_inv, parent_of):
    blocks = NC // CH_DEV

    def shape_blocks(a):
        return a.reshape((blocks, CH_DEV) + a.shape[1:])

    rhs_b = shape_blocks(child_rhs)
    linv_b = shape_blocks(child_lower_inv)
    loff_b = shape_blocks(child_lower_off)
    uinv_b = shape_blocks(child_upper_inv)
    uoff_b = shape_blocks(child_upper_off)
    owner_b = shape_blocks(parent_of)
    labels = jnp.arange(NP, dtype=jnp.int32)

    def forward(total, items):
        rhs, linv, loff, owner = items
        fwd = bmm(linv, rhs).astype(jnp.bfloat16)
        contrib = bmm(loff, fwd)
        onehot = (owner[:, None] == labels[None, :]).astype(jnp.float32)
        total = total + jnp.einsum('cp,cwr->pwr', onehot, contrib, precision=lax.Precision.HIGHEST)
        return total, fwd

    update, fwd_b = lax.scan(forward, jnp.zeros((NP, W, R), jnp.float32), (rhs_b, linv_b, loff_b, owner_b))
    parent_residual = (parent_rhs.astype(jnp.float32) - update).astype(jnp.bfloat16)
    parent_forward = bmm(parent_lower_inv, parent_residual).astype(jnp.bfloat16)
    parent_solution = bmm(parent_upper_inv, parent_forward).astype(jnp.bfloat16)

    def backward(items):
        fwd, uinv, uoff, owner = items
        picked = parent_solution[owner.astype(jnp.int32)]
        resid = (fwd.astype(jnp.float32) - bmm(uoff, picked)).astype(jnp.bfloat16)
        return bmm(uinv, resid).astype(jnp.bfloat16)

    child_solution = lax.map(backward, (fwd_b, uinv_b, uoff_b, owner_b))
    return child_solution.reshape(NC, W, R), parent_solution
```

```python
import functools

import jax
import jax.numpy as jnp
from jax import lax
from jax.experimental import pallas as pl
from jax.experimental.pallas import tpu as pltpu
from jax.sharding import PartitionSpec as P

BF = jnp.bfloat16
F32 = jnp.float32
MESH = pl.DeviceIdType.MESH
NCH = 48
GRP = 8
CHUNKS = NCH // GRP
NT = (((1,), (1,)), ((), ()))
TN = (((0,), (1,)), ((), ()))


def mm(a, b):
    return jnp.dot(a, b, preferred_element_type=F32)


def mm_nt(a, b):
    return lax.dot_general(a, b, NT, preferred_element_type=F32)


def loop(n, body, unroll=1):
    def step(i, carry):
        body(i)
        return carry

    lax.fori_loop(0, n, step, 0, unroll=unroll)


def kernel(
    tbl,
    po,
    rhs_h,
    prhs_h,
    linv_h,
    loff_h,
    uinv_h,
    uoff_h,
    plinv_h,
    puinv_h,
    out_h,
    psol_h,
    rhs,
    linv,
    loff,
    uinv,
    uoff,
    prhs,
    plinv,
    puinv,
    fwd,
    run,
    own,
    sib,
    sibr,
    snd,
    r1p,
    r1m,
    fp,
    fm,
    snd2,
    r2p,
    r2m,
    gp,
    gm,
    snd3,
    zr,
    prt,
    gath,
    ufwd,
    mat,
    outv,
    psolv,
    load_sem,
    out_sem,
    send_sem,
    recv_sem,
):
    x = lax.axis_index("row")
    col = lax.axis_index("col")
    core = lax.rem(col, 2)
    z = lax.rem(lax.div(col, 2), 8)
    y = lax.div(col, 16)
    flip = 1 - core
    a = flip * x + core * y
    b = flip * y + core * x

    def at_ab(a_, b_):
        x_ = flip * a_ + core * b_
        y_ = flip * b_ + core * a_
        return (x_, y_ * 16 + z * 2 + core)

    ap, am, ao = lax.rem(a + 1, 4), lax.rem(a + 3, 4), lax.rem(a + 2, 4)
    bp, bm, bo = lax.rem(b + 1, 4), lax.rem(b + 3, 4), lax.rem(b + 2, 4)
    d_ap, d_am, d_bp, d_bm = at_ab(ap, b), at_ab(am, b), at_ab(a, bp), at_ab(a, bm)
    d_sib = (x, y * 16 + z * 2 + flip)
    zs = [lax.rem(z + d, 8) for d in range(8)]
    d_z = [(x, y * 16 + zs[d] * 2 + core) for d in range(8)]

    barrier = pltpu.get_barrier_semaphore()
    peers = [d_sib, d_ap, d_am, d_bp, d_bm] + d_z[1:]
    for peer in peers:
        pl.semaphore_signal(barrier, inc=1, device_id=peer, device_id_type=MESH)

    loads = []

    def load(src, dst):
        cp = pltpu.make_async_copy(src, dst, load_sem.at[len(loads)])
        cp.start()
        loads.append(cp)
        return cp

    chunk_loads = []
    for k in range(CHUNKS):
        part = pl.ds(k * GRP, GRP)
        chunk_loads.append(
            [
                load(linv_h.at[part], linv.at[part]),
                load(rhs_h.at[part], rhs.at[part]),
                load(loff_h.at[part], loff.at[part]),
            ]
        )
    parent_loads = [load(prhs_h, prhs), load(plinv_h, plinv), load(puinv_h, puinv)]
    upper_loads = [load(uinv_h, uinv), load(uoff_h, uoff)]

    run[NCH] = jnp.zeros((128, 128), F32)

    for k in range(CHUNKS):
        for cp in chunk_loads[k]:
            cp.wait()

        def forward(i, k=k):
            c0 = k * GRP + i * 4
            terms = []
            for j in range(4):
                f = mm(linv[c0 + j], rhs[c0 + j]).astype(BF)
                fwd[c0 + j] = f
                terms.append(mm_nt(f.T, loff[c0 + j]))
            for j in range(4):
                run[c0 + j] = terms[j] + run[tbl[c0 + j]]

        loop(GRP // 4, forward)

    def place(h, j):
        yy, zz = lax.div(j, 8), lax.rem(j, 8)
        base = (1 - h) * j + h * (yy * 32 + zz)
        stride = (1 - h) * 32 + h * 8
        return base, stride

    def pack(h, ref, dtype):
        def body(j):
            v = run[tbl[NCH + 2 * j + h]]
            base, stride = place(h, j)
            for q in range(4):
                ref[base + q * stride] = v[32 * q : 32 * q + 32].astype(dtype)

        loop(32, body, unroll=2)

    pack(flip, sib, BF)
    pl.semaphore_wait(barrier, len(peers))

    sends = []

    def remote(src, dst, slot, dev):
        return pltpu.make_async_remote_copy(
            src_ref=src,
            dst_ref=dst,
            send_sem=send_sem.at[slot],
            recv_sem=recv_sem.at[slot],
            device_id=dev,
            device_id_type=MESH,
        )

    def send(src, dst, slot, dev):
        cp = remote(src, dst, slot, dev)
        cp.start()
        sends.append(cp)

    def arrived(dst, slot):
        remote(dst, dst, slot, d_sib).wait_recv()

    def half(i, h):
        return pl.ds(i * 32 + h * 16, 16)

    order = lambda m: [
        (lax.rem(m + 2, 4), 0),
        (lax.rem(m + 2, 4), 1),
        (lax.rem(m + 1, 4), 1),
        (lax.rem(m + 3, 4), 0),
        (lax.rem(m + 1, 4), 0),
        (lax.rem(m + 3, 4), 1),
        (m, 0),
        (m, 1),
    ]
    for s, (i, h) in enumerate(order(b)):
        send(sib.at[half(i, h)], sibr.at[half(i, h)], s, d_sib)
    pack(core, own, F32)

    def from_sib(s):
        i, h = order(a)[s]
        arrived(sibr.at[half(i, h)], s)

    def joined(i, h, more=None):
        def body(n):
            u = i * 32 + h * 16 + n
            v = own[u] + sibr[u].astype(F32)
            if more is not None:
                v = v + more[n].astype(F32)
            snd[u] = v.astype(BF)

        loop(16, body, unroll=4)

    A, B = pl.ds(0, 16), pl.ds(16, 16)
    from_sib(0)
    joined(ao, 0)
    send(snd.at[half(ao, 0)], r1p, 8, d_ap)
    from_sib(1)
    joined(ao, 1)
    send(snd.at[half(ao, 1)], r1m, 9, d_am)
    from_sib(2)
    joined(ap, 1)
    send(snd.at[half(ap, 1)], fp.at[B], 10, d_ap)
    from_sib(3)
    joined(am, 0)
    send(snd.at[half(am, 0)], fm.at[A], 11, d_am)
    from_sib(4)
    arrived(r1p, 8)
    joined(ap, 0, r1p)
    send(snd.at[half(ap, 0)], fp.at[A], 12, d_ap)
    from_sib(5)
    arrived(r1m, 9)
    joined(am, 1, r1m)
    send(snd.at[half(am, 1)], fm.at[B], 13, d_am)
    from_sib(6)
    from_sib(7)
    arrived(fp.at[B], 10)
    arrived(fm.at[A], 11)
    arrived(fp.at[A], 12)
    arrived(fm.at[B], 13)

    def at_a(n):
        u = a * 32 + n
        return own[u] + sibr[u].astype(F32) + fp[n].astype(F32) + fm[n].astype(F32)

    def half2(i, h):
        return pl.ds(i * 8 + h * 4, 4)

    def joined2(i, h, more=None):
        for n in range(4):
            u = i * 8 + h * 4 + n
            v = at_a(u)
            if more is not None:
                v = v + more[n].astype(F32)
            snd2[u] = v.astype(BF)

    A2, B2 = pl.ds(0, 4), pl.ds(4, 4)
    joined2(bo, 0)
    send(snd2.at[half2(bo, 0)], r2p, 14, d_bp)
    joined2(bo, 1)
    send(snd2.at[half2(bo, 1)], r2m, 15, d_bm)
    joined2(bp, 1)
    send(snd2.at[half2(bp, 1)], gp.at[B2], 16, d_bp)
    joined2(bm, 0)
    send(snd2.at[half2(bm, 0)], gm.at[A2], 17, d_bm)
    arrived(r2p, 14)
    joined2(bp, 0, r2p)
    send(snd2.at[half2(bp, 0)], gp.at[A2], 18, d_bp)
    arrived(r2m, 15)
    joined2(bm, 1, r2m)
    send(snd2.at[half2(bm, 1)], gm.at[B2], 19, d_bm)
    arrived(gp.at[B2], 16)
    arrived(gm.at[A2], 17)
    arrived(gp.at[A2], 18)
    arrived(gm.at[B2], 19)

    def at_b(i):
        return at_a(b * 8 + i) + gp[i].astype(F32) + gm[i].astype(F32)

    for d in (4, 3, 5, 2, 6, 1, 7):
        snd3[d - 1] = at_b(zs[d]).astype(BF)
        send(snd3.at[d - 1], zr.at[d - 1], 20 + d - 1, d_z[d])

    for cp in parent_loads:
        cp.wait()
    prt[...] = prhs[0].astype(F32).T
    for cp in upper_loads:
        cp.wait()

    def prepare(i):
        for j in range(4):
            c = i * 4 + j
            ui = uinv[c]
            ufwd[c] = mm(ui, fwd[c])
            mat[c] = mm(ui, uoff[c]).astype(BF)

    loop(NCH // 4, prepare)

    total = at_b(z)
    for d in range(1, 8):
        arrived(zr.at[d - 1], 20 + d - 1)
        total = total + zr[d - 1].astype(F32)

    res = (prt[pl.ds(x * 32, 32), :] - total).astype(BF)
    pf = mm_nt(res, plinv[0]).astype(BF)
    base = core * 128
    me = base + a * 32 + b * 8 + z
    gath[me] = mm_nt(pf, puinv[0]).astype(BF)

    for d in (4, 3, 5, 2, 6, 1, 7):
        send(gath.at[me], gath.at[me], 27 + d - 1, d_z[d])
    for d in range(1, 8):
        arrived(gath.at[base + a * 32 + b * 8 + zs[8 - d]], 27 + d - 1)

    def both(ref_slice, slot, dev):
        send(gath.at[ref_slice], gath.at[ref_slice], slot, dev)

    def bsl(i, start=0, n=8):
        return pl.ds(base + a * 32 + i * 8 + start, n)

    both(bsl(b), 34, d_bp)
    both(bsl(b), 35, d_bm)
    arrived(gath.at[bsl(bm)], 34)
    both(bsl(bm, 0, 4), 36, d_bp)
    arrived(gath.at[bsl(bp)], 35)
    both(bsl(bp, 4, 4), 37, d_bm)
    arrived(gath.at[bsl(bo, 0, 4)], 36)
    arrived(gath.at[bsl(bo, 4, 4)], 37)

    def asl(i, start=0, n=32, bs=base):
        return pl.ds(bs + i * 32 + start, n)

    both(asl(a), 38, d_ap)
    both(asl(a), 39, d_am)
    both(asl(a), 42, d_sib)
    arrived(gath.at[asl(am)], 38)
    both(asl(am, 0, 16), 40, d_ap)
    both(asl(am), 43, d_sib)
    arrived(gath.at[asl(ap)], 39)
    both(asl(ap, 16, 16), 41, d_am)
    both(asl(ap), 44, d_sib)
    arrived(gath.at[asl(ao, 0, 16)], 40)
    both(asl(ao, 0, 16), 45, d_sib)
    arrived(gath.at[asl(ao, 16, 16)], 41)
    both(asl(ao, 16, 16), 46, d_sib)
    other = flip * 128
    arrived(gath.at[asl(b, bs=other)], 42)
    arrived(gath.at[asl(bm, bs=other)], 43)
    arrived(gath.at[asl(bp, bs=other)], 44)
    arrived(gath.at[asl(bo, 0, 16, other)], 45)
    arrived(gath.at[asl(bo, 16, 16, other)], 46)

    def parent(p):
        h = lax.rem(p, 2)
        first, stride = place(h, lax.div(p, 2))
        return jnp.concatenate(
            [gath[h * 128 + first + q * stride] for q in range(4)], axis=0
        )

    psolv[0] = parent(col).T
    pcopy = pltpu.make_async_copy(psolv, psol_h, out_sem.at[CHUNKS])
    pcopy.start()

    copies = [pcopy]
    for k in range(CHUNKS):

        def backward(i, k=k):
            for j in range(4):
                c = k * GRP + i * 4 + j
                outv[c] = (ufwd[c] - mm_nt(mat[c], parent(po[c]))).astype(BF)

        loop(GRP // 4, backward)
        part = pl.ds(k * GRP, GRP)
        cp = pltpu.make_async_copy(outv.at[part], out_h.at[part], out_sem.at[k])
        cp.start()
        copies.append(cp)
    for cp in sends:
        cp.wait_send()
    for cp in copies:
        cp.wait()


def on_device(
    child_rhs,
    parent_rhs,
    child_lower_inv,
    child_lower_off,
    child_upper_inv,
    child_upper_off,
    parent_lower_inv,
    parent_upper_inv,
    parent_of,
):
    n = child_rhs.shape[0]
    n_par = 64
    ids = jnp.arange(n, dtype=jnp.int32)
    label = jnp.concatenate([parent_of, jnp.arange(n_par, dtype=jnp.int32)])
    limit = jnp.concatenate([ids, jnp.full((n_par,), n, jnp.int32)])
    hit = (label[:, None] == parent_of[None, :]) & (ids[None, :] < limit[:, None])
    last = jnp.max(jnp.where(hit, ids[None, :], -1), axis=1)
    tbl = jnp.where(last < 0, n, last)

    mats = lambda: pltpu.VMEM((NCH, 128, 128), BF)
    one = lambda: pltpu.VMEM((1, 128, 128), BF)
    units = lambda k, dtype=BF: pltpu.VMEM((k, 32, 128), dtype)
    smem = pl.BlockSpec(memory_space=pltpu.SMEM)
    hbm = pl.BlockSpec(memory_space=pl.ANY)
    return pl.pallas_call(
        kernel,
        out_shape=(
            jax.ShapeDtypeStruct(child_rhs.shape, BF),
            jax.ShapeDtypeStruct(parent_rhs.shape, BF),
        ),
        in_specs=[smem, smem] + [hbm] * 8,
        out_specs=(hbm, hbm),
        scratch_shapes=[
            mats(),
            mats(),
            mats(),
            mats(),
            mats(),
            one(),
            one(),
            one(),
            mats(),
            pltpu.VMEM((NCH + 1, 128, 128), F32),
            units(128, F32),
            units(128),
            units(128),
            units(128),
            units(16),
            units(16),
            units(32),
            units(32),
            units(32),
            units(4),
            units(4),
            units(8),
            units(8),
            units(7),
            units(7),
            pltpu.VMEM((128, 128), F32),
            units(256),
            pltpu.VMEM((NCH, 128, 128), F32),
            mats(),
            mats(),
            one(),
            pltpu.SemaphoreType.DMA((3 * CHUNKS + 5,)),
            pltpu.SemaphoreType.DMA((CHUNKS + 1,)),
            pltpu.SemaphoreType.DMA((47,)),
            pltpu.SemaphoreType.DMA((47,)),
        ],
        compiler_params=pltpu.CompilerParams(
            collective_id=0, has_side_effects=True, vmem_limit_bytes=60 * 2**20
        ),
    )(
        tbl,
        parent_of,
        child_rhs,
        parent_rhs,
        child_lower_inv,
        child_lower_off,
        child_upper_inv,
        child_upper_off,
        parent_lower_inv,
        parent_upper_inv,
    )


def solution(mesh):
    child = P(("row", "col"), None, None)
    par = P("col", None, None)
    return jax.shard_map(
        on_device,
        mesh=mesh,
        in_specs=(child, par, child, child, child, child, par, par, P(("row", "col"))),
        out_specs=(child, par),
        check_vma=False,
    )
```

```python
import jax
import jax.numpy as jnp
from jax import lax
from jax.experimental import pallas as pl
from jax.experimental.pallas import tpu as pltpu
from jax.sharding import PartitionSpec as P

BF = jnp.bfloat16
F32 = jnp.float32
MESH = pl.DeviceIdType.MESH
NCH = 48
GRP = 8
CHUNKS = NCH // GRP
NT = (((1,), (1,)), ((), ()))


def mm(a, b):
    return jnp.dot(a, b, preferred_element_type=F32)


def mm_nt(a, b):
    return lax.dot_general(a, b, NT, preferred_element_type=F32)


def loop(n, body, unroll=1):
    def step(i, carry):
        body(i)
        return carry

    lax.fori_loop(0, n, step, 0, unroll=unroll)


def forward_kernel(
    po_h,
    rhs_h,
    prhs_h,
    linv_h,
    loff_h,
    uinv_h,
    uoff_h,
    plinv_h,
    puinv_h,
    gath,
    ufwd,
    mat,
    rhs,
    linv,
    loff,
    uinv,
    uoff,
    prhs,
    plinv,
    puinv,
    fwd,
    run,
    pov,
    tabv,
    tab,
    sib,
    sibr,
    snd,
    r1,
    fin,
    snd2,
    gin,
    snd3,
    zr_out,
    zr,
    prt,
    load_sem,
    tab_sem,
    send_sem,
    recv_sem,
):
    x = lax.axis_index("row")
    col = lax.axis_index("col")
    core = lax.rem(col, 2)
    z = lax.rem(lax.div(col, 2), 8)
    y = lax.div(col, 16)
    flip = 1 - core

    def dev(x_, y_, z_, c_):
        return (x_, y_ * 16 + z_ * 2 + c_)

    def mod4(v):
        return lax.rem(v, 4)

    d_sib = dev(x, y, z, flip)
    d_x = [dev(mod4(x + d), y, z, core) for d in range(4)]
    d_y = [dev(x, mod4(y + d), z, core) for d in range(4)]
    zs = [lax.rem(z + d, 8) for d in range(8)]
    d_z = [dev(x, y, zs[d], core) for d in range(8)]
    d_a, d_b = (d_x, d_y), (d_y, d_x)
    ax = [[mod4(x + d) for d in range(4)], [mod4(y + d) for d in range(4)]]
    bx = [ax[1], ax[0]]

    barrier = pltpu.get_barrier_semaphore()
    peers = [d_sib] + d_x[1:] + d_y[1:] + d_z[1:]
    for peer in peers:
        pl.semaphore_signal(barrier, inc=1, device_id=peer, device_id_type=MESH)

    loads, sends, pend = [], [], {}

    def load(src, dst):
        cp = pltpu.make_async_copy(src, dst, load_sem.at[len(loads)])
        cp.start()
        loads.append(cp)
        return cp

    po_load = load(po_h, pov)
    chunk_loads = []
    for k in range(CHUNKS):
        part = pl.ds(k * GRP, GRP)
        chunk_loads.append(
            [
                load(linv_h.at[part], linv.at[part]),
                load(rhs_h.at[part], rhs.at[part]),
                load(loff_h.at[part], loff.at[part]),
            ]
        )
    parent_loads = [load(prhs_h, prhs), load(plinv_h, plinv), load(puinv_h, puinv)]
    upper_loads = [load(uinv_h, uinv), load(uoff_h, uoff)]

    run[NCH] = jnp.zeros((128, 128), F32)

    po_load.wait()
    mine = jnp.concatenate(
        [pov[...], jnp.full((1, 128 - NCH), -1, jnp.int32)], axis=1
    )
    rows = jnp.broadcast_to(mine, (128, 128))
    lane = lax.broadcasted_iota(jnp.int32, (128, 128), 1)
    child = lax.broadcasted_iota(jnp.int32, (128, 128), 0)
    label = jnp.where(lane < 64, rows, lane - 64)
    hit = (rows.T == label) & (child < jnp.where(lane < 64, lane, NCH))
    last = jnp.max(jnp.where(hit, child, -1), axis=0, keepdims=True)
    tabv[...] = jnp.where(last < 0, NCH, last)
    tab_copy = pltpu.make_async_copy(tabv, tab, tab_sem.at[0])
    tab_copy.start()

    for k in range(CHUNKS):
        for cp in chunk_loads[k]:
            cp.wait()
        terms = []
        for c in range(k * GRP, (k + 1) * GRP):
            f = mm(linv[c], rhs[c]).astype(BF)
            fwd[c] = f
            terms.append(mm_nt(f.T, loff[c]))
        if k == 0:
            tab_copy.wait()
        for j in range(GRP):
            c = k * GRP + j
            run[c] = terms[j] + run[tab[0, c]]

    def mine_of(t, i, h, n, core_):
        b_, zz = h * 2 + lax.div(n, 4), t * 4 + lax.rem(n, 4)
        x_, y_ = (i, b_) if t == 0 else (b_, i)
        row = pl.multiple_of(x_ * 32, 32)
        last_ = tab[0, 64 + y_ * 16 + zz * 2 + core_]
        return run[last_, pl.ds(row, 32), :]

    def remote(src, dst, slot, dev_):
        return pltpu.make_async_remote_copy(
            src_ref=src,
            dst_ref=dst,
            send_sem=send_sem.at[slot],
            recv_sem=recv_sem.at[slot],
            device_id=dev_,
            device_id_type=MESH,
        )

    def send(src, dst, slot, dev_):
        cp = remote(src, dst, slot, dev_)
        cp.start()
        sends.append(cp)
        pend[slot] = src

    def arrived(dst, slot):
        remote(dst, dst, slot, d_sib).wait_recv()
        pend.pop(slot)

    slots = {}

    def slot(*key):
        return slots.setdefault(key, len(slots))

    def half(i, h):
        return pl.ds(i * 16 + h * 8, 8)

    both = (0, 1)
    order = [(2, 0), (2, 1), (1, 1), (3, 0), (1, 0), (3, 1), (0, 0), (0, 1)]

    for s, (d, h) in enumerate(order):
        for t in both:
            i = ax[t][d]

            def pack(n, t=t, i=i, h=h):
                u = i * 16 + h * 8 + n
                sib[t, u] = mine_of(t, i, h, n, flip).astype(BF)

            loop(8, pack, unroll=8)
            if s == 0 and t == 0:
                pl.semaphore_wait(barrier, len(peers))
            send(
                sib.at[t, half(i, h)], sibr.at[t, half(i, h)], slot("s0", t, s), d_sib
            )

    def from_sib(t, s):
        d, h = order[s]
        arrived(sibr.at[t, half(ax[t][d], h)], slot("s0", t, s))

    def joined(t, d, h, more=None):
        i = ax[t][d]

        def body(n):
            u = i * 16 + h * 8 + n
            v = mine_of(t, i, h, n, core) + sibr[t, u].astype(F32)
            if more is not None:
                v = v + more[n].astype(F32)
            snd[t, u] = v.astype(BF)

        loop(8, body, unroll=8)
        return snd.at[t, half(i, h)]

    H = [pl.ds(0, 8), pl.ds(8, 8)]
    for t in both:
        from_sib(t, 0)
        send(joined(t, 2, 0), r1.at[t, 0], slot("r1", t, 0), d_a[t][1])
        from_sib(t, 1)
        send(joined(t, 2, 1), r1.at[t, 1], slot("r1", t, 1), d_a[t][3])
    for t in both:
        from_sib(t, 2)
        send(joined(t, 1, 1), fin.at[t, 0, H[1]], slot("f", t, 0, 1), d_a[t][1])
        from_sib(t, 3)
        send(joined(t, 3, 0), fin.at[t, 1, H[0]], slot("f", t, 1, 0), d_a[t][3])
    for t in both:
        for s in (4, 5):
            from_sib(t, s)
    for t in both:
        arrived(r1.at[t, 0], slot("r1", t, 0))
        src = joined(t, 1, 0, r1.at[t, 0])
        send(src, fin.at[t, 0, H[0]], slot("f", t, 0, 0), d_a[t][1])
        arrived(r1.at[t, 1], slot("r1", t, 1))
        src = joined(t, 3, 1, r1.at[t, 1])
        send(src, fin.at[t, 1, H[1]], slot("f", t, 1, 1), d_a[t][3])
    for t in both:
        for s in (6, 7):
            from_sib(t, s)
    for t in both:
        arrived(fin.at[t, 0, H[1]], slot("f", t, 0, 1))
        arrived(fin.at[t, 1, H[0]], slot("f", t, 1, 0))

    def at_a(t, b_, zz):
        n = b_ * 4 + zz
        v = mine_of(t, ax[t][0], 0, n, core) + sibr[t, ax[t][0] * 16 + n].astype(F32)
        return v + fin[t, 0, n].astype(F32) + fin[t, 1, n].astype(F32)

    for t in both:
        arrived(fin.at[t, 0, H[0]], slot("f", t, 0, 0))
        arrived(fin.at[t, 1, H[1]], slot("f", t, 1, 1))
        for d in (2, 1, 3):
            for zz in range(4):
                snd2[t, d - 1, zz] = at_a(t, bx[t][d], zz).astype(BF)
            send(snd2.at[t, d - 1], gin.at[t, d - 1], slot("g", t, d), d_b[t][d])

    def at_b(t, zz):
        v = at_a(t, bx[t][0], zz)
        for d in range(3):
            v = v + gin[t, d, zz].astype(F32)
        return v

    near = lax.div(z, 4)
    tot = []
    for t in both:
        for d in (2, 1, 3):
            arrived(gin.at[t, d - 1], slot("g", t, d))
        for zz in range(4):
            snd3[t * 4 + zz] = at_b(t, zz)
    for d in (4, 3, 5, 2, 6, 1, 7):
        zr_out[d - 1] = snd3[zs[d]].astype(BF)
        send(zr_out.at[d - 1], zr.at[d - 1], slot("z", d), d_z[d])

    for cp in parent_loads:
        cp.wait()
    prt[...] = prhs[0].astype(F32).T
    for cp in upper_loads:
        cp.wait()

    def prepare(i):
        for j in range(4):
            c = i * 4 + j
            ui = uinv[c]
            ufwd[c] = mm(ui, fwd[c])
            mat[c] = mm(ui, uoff[c]).astype(BF)

    loop(NCH // 4, prepare)

    total = snd3[z]
    for d in range(1, 8):
        arrived(zr.at[d - 1], slot("z", d))
        total = total + zr[d - 1].astype(F32)

    res = (prt[pl.ds(pl.multiple_of(x * 32, 32), 32), :] - total).astype(BF)
    pf = mm_nt(res, plinv[0]).astype(BF)

    def unit(z_):
        t_ = lax.div(z_, 4)
        ab = (1 - t_) * (x * 4 + y) + t_ * (y * 4 + x)
        return (core * 2 + t_) * 64 + ab * 4 + lax.rem(z_, 4)

    me = unit(z)
    gath[me] = mm_nt(pf, puinv[0]).astype(BF)

    for d in (4, 3, 5, 2, 6, 1, 7):
        send(gath.at[me], gath.at[me], slot("bz", d), d_z[d])
    for d in (7, 1, 6, 2, 5, 3, 4):
        arrived(gath.at[unit(zs[8 - d])], slot("bz", d))

    def share(ref_slice, slot_, dev_):
        send(gath.at[ref_slice], gath.at[ref_slice], slot_, dev_)

    def bsl(t, d):
        return pl.ds((core * 2 + t) * 64 + ax[t][0] * 16 + bx[t][d] * 4, 4)

    for t in both:
        for d in (2, 1, 3):
            share(bsl(t, 0), slot("bb", t, d), d_b[t][d])
    for d in (1, 3, 2):
        for t in both:
            arrived(gath.at[bsl(t, 4 - d)], slot("bb", t, d))

    def asl(t, d, h, core_=core):
        return pl.ds((core_ * 2 + t) * 64 + ax[t][d] * 16 + h * 8, 8)

    def over(t, d, h):
        share(asl(t, d, h), slot("o", t, d, h), d_sib)

    for t in both:
        share(asl(t, 0, 0), slot("ba", t, 1, 0), d_a[t][1])
        share(asl(t, 0, 1), slot("ba", t, 3, 1), d_a[t][3])
    for t in both:
        share(asl(t, 0, 1), slot("ba", t, 1, 1), d_a[t][1])
        share(asl(t, 0, 0), slot("ba", t, 3, 0), d_a[t][3])
    for t in both:
        for h in (0, 1):
            over(t, 0, h)
    for t in both:
        arrived(gath.at[asl(t, 3, 0)], slot("ba", t, 1, 0))
        share(asl(t, 3, 0), slot("ba", t, 2, 0), d_a[t][1])
        arrived(gath.at[asl(t, 1, 1)], slot("ba", t, 3, 1))
        share(asl(t, 1, 1), slot("ba", t, 2, 1), d_a[t][3])
    for t in both:
        over(t, 3, 0)
        over(t, 1, 1)
    for t in both:
        arrived(gath.at[asl(t, 3, 1)], slot("ba", t, 1, 1))
        over(t, 3, 1)
        arrived(gath.at[asl(t, 1, 0)], slot("ba", t, 3, 0))
        over(t, 1, 0)
    for h in (0, 1):
        for t in both:
            arrived(gath.at[asl(t, 2, h)], slot("ba", t, 2, h))
            over(t, 2, h)
    for d in (0, 3, 1, 2):
        for h in (0, 1):
            for t in both:
                arrived(gath.at[asl(t, d, h, flip)], slot("o", t, d, h))
    for cp in sends:
        cp.wait_send()


def parent_of_units(gath, p):
    h, z, y = lax.rem(p, 2), lax.rem(lax.div(p, 2), 8), lax.div(p, 16)
    t = lax.div(z, 4)
    first = (h * 2 + t) * 64 + lax.rem(z, 4) + (1 - t) * y * 4 + t * y * 16
    stride = (1 - t) * 16 + t * 4
    return jnp.concatenate([gath[first + q * stride] for q in range(4)], axis=0)


def backward_kernel(po, gath, ufwd, mat, out_h, psol_h, out, psol, sem):
    psol[0] = parent_of_units(gath, lax.axis_index("col")).T
    copies = []

    def put(src, dst):
        cp = pltpu.make_async_copy(src, dst, sem.at[len(copies)])
        cp.start()
        copies.append(cp)

    put(psol, psol_h)
    for k in range(CHUNKS):
        for c in range(k * GRP, (k + 1) * GRP):
            s = parent_of_units(gath, po[c])
            out[c] = (ufwd[c] - mm_nt(mat[c], s)).astype(BF)
        part = pl.ds(k * GRP, GRP)
        put(out.at[part], out_h.at[part])
    for cp in copies:
        cp.wait()


def on_device(
    child_rhs,
    parent_rhs,
    child_lower_inv,
    child_lower_off,
    child_upper_inv,
    child_upper_off,
    parent_lower_inv,
    parent_upper_inv,
    parent_of,
):
    mats = lambda: pltpu.VMEM((NCH, 128, 128), BF)
    one = lambda: pltpu.VMEM((1, 128, 128), BF)
    units = lambda *k: pltpu.VMEM((*k, 32, 128), BF)
    smem = pl.BlockSpec(memory_space=pltpu.SMEM)
    vmem = pl.BlockSpec(memory_space=pltpu.VMEM)
    hbm = pl.BlockSpec(memory_space=pl.ANY)
    gath, ufwd, mat = pl.pallas_call(
        forward_kernel,
        out_shape=(
            jax.ShapeDtypeStruct((256, 32, 128), BF),
            jax.ShapeDtypeStruct((NCH, 128, 128), F32),
            jax.ShapeDtypeStruct((NCH, 128, 128), BF),
        ),
        in_specs=[hbm] * 9,
        out_specs=(vmem, vmem, vmem),
        scratch_shapes=[
            mats(),
            mats(),
            mats(),
            mats(),
            mats(),
            one(),
            one(),
            one(),
            mats(),
            pltpu.VMEM((NCH + 1, 128, 128), F32),
            pltpu.VMEM((1, NCH), jnp.int32),
            pltpu.VMEM((1, 128), jnp.int32),
            pltpu.SMEM((1, 128), jnp.int32),
            units(2, 64),
            units(2, 64),
            units(2, 64),
            units(2, 2, 8),
            units(2, 2, 16),
            units(2, 3, 4),
            units(2, 3, 4),
            pltpu.VMEM((8, 32, 128), F32),
            units(7),
            units(7),
            pltpu.VMEM((128, 128), F32),
            pltpu.SemaphoreType.DMA((3 * CHUNKS + 6,)),
            pltpu.SemaphoreType.DMA((1,)),
            pltpu.SemaphoreType.DMA((90,)),
            pltpu.SemaphoreType.DMA((90,)),
        ],
        compiler_params=pltpu.CompilerParams(
            collective_id=0, has_side_effects=True, vmem_limit_bytes=40 * 2**20
        ),
    )(
        *[
            pltpu.with_memory_space_constraint(v, pltpu.HBM)
            for v in (
                parent_of.reshape(1, NCH),
                child_rhs,
                parent_rhs,
                child_lower_inv,
                child_lower_off,
                child_upper_inv,
                child_upper_off,
                parent_lower_inv,
                parent_upper_inv,
            )
        ]
    )
    return pl.pallas_call(
        backward_kernel,
        out_shape=(
            jax.ShapeDtypeStruct(child_rhs.shape, BF),
            jax.ShapeDtypeStruct(parent_rhs.shape, BF),
        ),
        in_specs=[smem, vmem, vmem, vmem],
        out_specs=(hbm, hbm),
        scratch_shapes=[mats(), one(), pltpu.SemaphoreType.DMA((CHUNKS + 1,))],
        compiler_params=pltpu.CompilerParams(vmem_limit_bytes=16 * 2**20),
    )(parent_of, gath, ufwd, mat)


def solution(mesh):
    child = P(("row", "col"), None, None)
    par = P("col", None, None)
    return jax.shard_map(
        on_device,
        mesh=mesh,
        in_specs=(child, par, child, child, child, child, par, par, P(("row", "col"))),
        out_specs=(child, par),
        check_vma=False,
    )
```

```python
import jax
import jax.numpy as jnp
from jax import lax
from jax.experimental import pallas as pl
from jax.experimental.pallas import tpu as pltpu
from jax.sharding import PartitionSpec as P

BF = jnp.bfloat16
F32 = jnp.float32
MESH = pl.DeviceIdType.MESH
NCH = 48
GRP = 8
CHUNKS = NCH // GRP
NT = (((1,), (1,)), ((), ()))


def mm(a, b):
    return jnp.dot(a, b, preferred_element_type=F32)


def mm_nt(a, b):
    return lax.dot_general(a, b, NT, preferred_element_type=F32)


def loop(n, body, unroll=1):
    def step(i, carry):
        body(i)
        return carry

    lax.fori_loop(0, n, step, 0, unroll=unroll)


def forward_kernel(
    po_h,
    rhs_h,
    prhs_h,
    linv_h,
    loff_h,
    uinv_h,
    uoff_h,
    plinv_h,
    puinv_h,
    gath,
    ufwd,
    mat,
    rhs,
    linv,
    loff,
    uinv,
    uoff,
    prhs,
    plinv,
    puinv,
    fwd,
    run,
    pov,
    tabv,
    tab,
    sib,
    sibr,
    snd,
    fin,
    snd2,
    gin,
    snd3,
    zr_out,
    zr,
    prt,
    load_sem,
    tab_sem,
    send_sem,
    recv_sem,
):
    x = lax.axis_index("row")
    col = lax.axis_index("col")
    core = lax.rem(col, 2)
    z = lax.rem(lax.div(col, 2), 8)
    y = lax.div(col, 16)
    flip = 1 - core

    def dev(x_, y_, z_, c_):
        return (x_, y_ * 16 + z_ * 2 + c_)

    def mod4(v):
        return lax.rem(v, 4)

    d_sib = dev(x, y, z, flip)
    d_x = [dev(mod4(x + d), y, z, core) for d in range(4)]
    d_y = [dev(x, mod4(y + d), z, core) for d in range(4)]
    zs = [lax.rem(z + d, 8) for d in range(8)]
    d_z = [dev(x, y, zs[d], core) for d in range(8)]
    d_a, d_b = (d_x, d_y), (d_y, d_x)
    ax = [[mod4(x + d) for d in range(4)], [mod4(y + d) for d in range(4)]]
    bx = [ax[1], ax[0]]

    barrier = pltpu.get_barrier_semaphore()
    peers = [d_sib] + d_x[1:] + d_y[1:] + d_z[1:]
    for peer in peers:
        pl.semaphore_signal(barrier, inc=1, device_id=peer, device_id_type=MESH)

    loads, sends, pend = [], [], {}

    def load(src, dst):
        cp = pltpu.make_async_copy(src, dst, load_sem.at[len(loads)])
        cp.start()
        loads.append(cp)
        return cp

    po_load = load(po_h, pov)
    chunk_loads = []
    for k in range(CHUNKS):
        part = pl.ds(k * GRP, GRP)
        chunk_loads.append(
            [
                load(linv_h.at[part], linv.at[part]),
                load(rhs_h.at[part], rhs.at[part]),
                load(loff_h.at[part], loff.at[part]),
            ]
        )
    parent_loads = [load(prhs_h, prhs), load(plinv_h, plinv), load(puinv_h, puinv)]
    upper_loads = [load(uinv_h, uinv), load(uoff_h, uoff)]

    run[NCH] = jnp.zeros((128, 128), F32)

    po_load.wait()
    mine = jnp.concatenate(
        [pov[...], jnp.full((1, 128 - NCH), -1, jnp.int32)], axis=1
    )
    rows = jnp.broadcast_to(mine, (128, 128))
    lane = lax.broadcasted_iota(jnp.int32, (128, 128), 1)
    child = lax.broadcasted_iota(jnp.int32, (128, 128), 0)
    label = jnp.where(lane < 64, rows, lane - 64)
    hit = (rows.T == label) & (child < jnp.where(lane < 64, lane, NCH))
    last = jnp.max(jnp.where(hit, child, -1), axis=0, keepdims=True)
    tabv[...] = jnp.where(last < 0, NCH, last)
    tab_copy = pltpu.make_async_copy(tabv, tab, tab_sem.at[0])
    tab_copy.start()

    for k in range(CHUNKS):
        for cp in chunk_loads[k]:
            cp.wait()
        terms = []
        for c in range(k * GRP, (k + 1) * GRP):
            f = mm(linv[c], rhs[c]).astype(BF)
            fwd[c] = f
            terms.append(mm_nt(f.T, loff[c]))
        if k == 0:
            tab_copy.wait()
        for j in range(GRP):
            c = k * GRP + j
            run[c] = terms[j] + run[tab[0, c]]

    def mine_of(t, b_, a_, zz, core_):
        x_, y_ = (a_, b_) if t == 0 else (b_, a_)
        row = pl.multiple_of(x_ * 32, 32)
        last_ = tab[0, 64 + y_ * 16 + (t * 4 + zz) * 2 + core_]
        return run[last_, pl.ds(row, 32), :]

    def remote(src, dst, slot, dev_):
        return pltpu.make_async_remote_copy(
            src_ref=src,
            dst_ref=dst,
            send_sem=send_sem.at[slot],
            recv_sem=recv_sem.at[slot],
            device_id=dev_,
            device_id_type=MESH,
        )

    def send(src, dst, slot, dev_):
        cp = remote(src, dst, slot, dev_)
        cp.start()
        sends.append(cp)
        pend[slot] = src

    def arrived(dst, slot):
        remote(dst, dst, slot, d_sib).wait_recv()
        pend.pop(slot)

    slots = {}

    def slot(*key):
        return slots.setdefault(key, len(slots))

    both = (0, 1)
    order = (2, 1, 3, 0)

    def row_of(b_):
        return pl.ds(b_ * 16, 16)

    waited = False
    for d in order:
        for t in both:
            b_ = bx[t][d]
            for a_ in range(4):
                for zz in range(4):
                    v = mine_of(t, b_, a_, zz, flip)
                    sib[t, b_ * 16 + a_ * 4 + zz] = v.astype(BF)
            if not waited:
                pl.semaphore_wait(barrier, len(peers))
                waited = True
            rows_ = row_of(b_)
            send(sib.at[t, rows_], sibr.at[t, rows_], slot("s0", t, d), d_sib)

    for e in order:
        for t in both:
            b_ = bx[t][e]
            arrived(sibr.at[t, row_of(b_)], slot("s0", t, e))
            for d in order[:3]:
                a_ = ax[t][d]
                for zz in range(4):
                    u = b_ * 16 + a_ * 4 + zz
                    v = mine_of(t, b_, a_, zz, core) + sibr[t, u].astype(F32)
                    snd[t, u] = v.astype(BF)
                src = snd.at[t, pl.ds(b_ * 16 + a_ * 4, 4)]
                send(src, fin.at[t, d - 1, e], slot("f", t, d, e), d_a[t][d])

    def at_a(t, e, zz):
        b_, a_ = bx[t][e], ax[t][0]
        v = mine_of(t, b_, a_, zz, core) + sibr[t, b_ * 16 + a_ * 4 + zz].astype(F32)
        for d in range(3):
            v = v + fin[t, d, e, zz].astype(F32)
        return v

    for e in order:
        for t in both:
            for d in order[:3]:
                arrived(fin.at[t, d - 1, e], slot("f", t, d, e))
            if e == 0:
                continue
            for zz in range(4):
                snd2[t, e - 1, zz] = at_a(t, e, zz).astype(BF)
            send(snd2.at[t, e - 1], gin.at[t, e - 1], slot("g", t, e), d_b[t][e])

    def at_b(t, zz):
        v = at_a(t, 0, zz)
        for d in range(3):
            v = v + gin[t, d, zz].astype(F32)
        return v

    for t in both:
        for d in (2, 1, 3):
            arrived(gin.at[t, d - 1], slot("g", t, d))
        for zz in range(4):
            snd3[t * 4 + zz] = at_b(t, zz)
    for d in (4, 3, 5, 2, 6, 1, 7):
        zr_out[d - 1] = snd3[zs[d]].astype(BF)
        send(zr_out.at[d - 1], zr.at[d - 1], slot("z", d), d_z[d])

    for cp in parent_loads:
        cp.wait()
    prt[...] = prhs[0].astype(F32).T
    for cp in upper_loads:
        cp.wait()

    def prepare(i):
        for j in range(4):
            c = i * 4 + j
            ui = uinv[c]
            ufwd[c] = mm(ui, fwd[c])
            mat[c] = mm(ui, uoff[c]).astype(BF)

    loop(NCH // 4, prepare)

    total = snd3[z]
    for d in range(1, 8):
        arrived(zr.at[d - 1], slot("z", d))
        total = total + zr[d - 1].astype(F32)

    res = (prt[pl.ds(pl.multiple_of(x * 32, 32), 32), :] - total).astype(BF)
    pf = mm_nt(res, plinv[0]).astype(BF)

    def unit(z_):
        t_ = lax.div(z_, 4)
        ab = (1 - t_) * (y * 4 + x) + t_ * (x * 4 + y)
        return (core * 2 + t_) * 64 + ab * 4 + lax.rem(z_, 4)

    me = unit(z)
    gath[me] = mm_nt(pf, puinv[0]).astype(BF)

    for d in (4, 3, 5, 2, 6, 1, 7):
        send(gath.at[me], gath.at[me], slot("bz", d), d_z[d])
    for d in (7, 1, 6, 2, 5, 3, 4):
        arrived(gath.at[unit(zs[8 - d])], slot("bz", d))

    def share(ref_slice, slot_, dev_):
        send(gath.at[ref_slice], gath.at[ref_slice], slot_, dev_)

    def piece(t, e, d, core_=core):
        return pl.ds((core_ * 2 + t) * 64 + bx[t][e] * 16 + ax[t][d] * 4, 4)

    def whole_row(t, e, core_=core):
        return pl.ds((core_ * 2 + t) * 64 + bx[t][e] * 16, 16)

    def along_a(t, e):
        for d in order[:3]:
            share(piece(t, e, 0), slot("ba", t, e, d), d_a[t][d])

    for t in both:
        for e in order[:3]:
            share(piece(t, 0, 0), slot("bb", t, e), d_b[t][e])
    for t in both:
        along_a(t, 0)
    for e in (1, 3, 2):
        for t in both:
            arrived(gath.at[piece(t, e, 0)], slot("bb", t, 4 - e))
            along_a(t, e)
    back = (0, 1, 3, 2)
    for e in back:
        for t in both:
            for d in back[1:]:
                arrived(gath.at[piece(t, e, d)], slot("ba", t, e, 4 - d))
            share(whole_row(t, e), slot("o", t, e), d_sib)
    for e in back:
        for t in both:
            arrived(gath.at[whole_row(t, e, flip)], slot("o", t, e))
    for cp in sends:
        cp.wait_send()


def parent_of_units(gath, p):
    h, z, y = lax.rem(p, 2), lax.rem(lax.div(p, 2), 8), lax.div(p, 16)
    t = lax.div(z, 4)
    first = (h * 2 + t) * 64 + lax.rem(z, 4) + (1 - t) * y * 16 + t * y * 4
    stride = (1 - t) * 4 + t * 16
    return jnp.concatenate([gath[first + q * stride] for q in range(4)], axis=0)


def backward_kernel(po, gath, ufwd, mat, out_h, psol_h, out, psol, sem):
    psol[0] = parent_of_units(gath, lax.axis_index("col")).T
    copies = []

    def put(src, dst):
        cp = pltpu.make_async_copy(src, dst, sem.at[len(copies)])
        cp.start()
        copies.append(cp)

    put(psol, psol_h)
    for k in range(CHUNKS):
        for c in range(k * GRP, (k + 1) * GRP):
            s = parent_of_units(gath, po[c])
            out[c] = (ufwd[c] - mm_nt(mat[c], s)).astype(BF)
        part = pl.ds(k * GRP, GRP)
        put(out.at[part], out_h.at[part])
    for cp in copies:
        cp.wait()


def on_device(
    child_rhs,
    parent_rhs,
    child_lower_inv,
    child_lower_off,
    child_upper_inv,
    child_upper_off,
    parent_lower_inv,
    parent_upper_inv,
    parent_of,
):
    mats = lambda: pltpu.VMEM((NCH, 128, 128), BF)
    one = lambda: pltpu.VMEM((1, 128, 128), BF)
    units = lambda *k: pltpu.VMEM((*k, 32, 128), BF)
    smem = pl.BlockSpec(memory_space=pltpu.SMEM)
    vmem = pl.BlockSpec(memory_space=pltpu.VMEM)
    hbm = pl.BlockSpec(memory_space=pl.ANY)
    gath, ufwd, mat = pl.pallas_call(
        forward_kernel,
        out_shape=(
            jax.ShapeDtypeStruct((256, 32, 128), BF),
            jax.ShapeDtypeStruct((NCH, 128, 128), F32),
            jax.ShapeDtypeStruct((NCH, 128, 128), BF),
        ),
        in_specs=[hbm] * 9,
        out_specs=(vmem, vmem, vmem),
        scratch_shapes=[
            mats(),
            mats(),
            mats(),
            mats(),
            mats(),
            one(),
            one(),
            one(),
            mats(),
            pltpu.VMEM((NCH + 1, 128, 128), F32),
            pltpu.VMEM((1, NCH), jnp.int32),
            pltpu.VMEM((1, 128), jnp.int32),
            pltpu.SMEM((1, 128), jnp.int32),
            units(2, 64),
            units(2, 64),
            units(2, 64),
            units(2, 3, 4, 4),
            units(2, 3, 4),
            units(2, 3, 4),
            pltpu.VMEM((8, 32, 128), F32),
            units(7),
            units(7),
            pltpu.VMEM((128, 128), F32),
            pltpu.SemaphoreType.DMA((3 * CHUNKS + 6,)),
            pltpu.SemaphoreType.DMA((1,)),
            pltpu.SemaphoreType.DMA((90,)),
            pltpu.SemaphoreType.DMA((90,)),
        ],
        compiler_params=pltpu.CompilerParams(
            collective_id=0, has_side_effects=True, vmem_limit_bytes=40 * 2**20
        ),
    )(
        *[
            pltpu.with_memory_space_constraint(v, pltpu.HBM)
            for v in (
                parent_of.reshape(1, NCH),
                child_rhs,
                parent_rhs,
                child_lower_inv,
                child_lower_off,
                child_upper_inv,
                child_upper_off,
                parent_lower_inv,
                parent_upper_inv,
            )
        ]
    )
    return pl.pallas_call(
        backward_kernel,
        out_shape=(
            jax.ShapeDtypeStruct(child_rhs.shape, BF),
            jax.ShapeDtypeStruct(parent_rhs.shape, BF),
        ),
        in_specs=[smem, vmem, vmem, vmem],
        out_specs=(hbm, hbm),
        scratch_shapes=[mats(), one(), pltpu.SemaphoreType.DMA((CHUNKS + 1,))],
        compiler_params=pltpu.CompilerParams(vmem_limit_bytes=16 * 2**20),
    )(parent_of, gath, ufwd, mat)


def solution(mesh):
    child = P(("row", "col"), None, None)
    par = P("col", None, None)
    return jax.shard_map(
        on_device,
        mesh=mesh,
        in_specs=(child, par, child, child, child, child, par, par, P(("row", "col"))),
        out_specs=(child, par),
        check_vma=False,
    )
```

```python
import jax
import jax.numpy as jnp
from jax import lax
from jax.experimental import pallas as pl
from jax.experimental.pallas import tpu as pltpu
from jax.sharding import PartitionSpec as P

BF = jnp.bfloat16
F32 = jnp.float32
MESH = pl.DeviceIdType.MESH
NCH = 48
GRP = 8
CHUNKS = NCH // GRP
NT = (((1,), (1,)), ((), ()))


def mm(a, b):
    return jnp.dot(a, b, preferred_element_type=F32)


def mm_nt(a, b):
    return lax.dot_general(a, b, NT, preferred_element_type=F32)


def loop(n, body, unroll=1):
    def step(i, carry):
        body(i)
        return carry

    lax.fori_loop(0, n, step, 0, unroll=unroll)


NEAR = (0, 1, 7, 2, 6, 3, 5, 4)
PARTS = range(4)


def place_of(p, z):
    h, pz, y = lax.rem(p, 2), lax.rem(lax.div(p, 2), 8), lax.div(p, 16)
    far = lax.rem(pz - z + 8, 8)
    pos = jnp.maximum(jnp.minimum(2 * far - 1, 16 - 2 * far), 0)
    t, odd = lax.div(pos, 2), lax.rem(lax.div(pos, 2), 2)
    first = (h * 4 + t) * 32 + lax.rem(pos, 2) + (1 - odd) * y * 8 + odd * y * 2
    return first, (1 - odd) * 2 + odd * 8


def parent_of_units(gath, p, z):
    first, step = place_of(p, z)
    return jnp.concatenate([gath[first + q * step] for q in range(4)], axis=0)


def forward_kernel(
    po_h,
    rhs_h,
    prhs_h,
    linv_h,
    loff_h,
    uinv_h,
    uoff_h,
    plinv_h,
    puinv_h,
    gath,
    ufwd,
    mat,
    rhs,
    linv,
    loff,
    uinv,
    uoff,
    prhs,
    plinv,
    puinv,
    fwd,
    run,
    pov,
    tabv,
    tab,
    sib,
    sibr,
    snd,
    fin,
    snd2,
    gin,
    held,
    zr_out,
    zr,
    sol,
    prt,
    load_sem,
    tab_sem,
    send_sem,
    recv_sem,
):
    x = lax.axis_index("row")
    col = lax.axis_index("col")
    core = lax.rem(col, 2)
    z = lax.rem(lax.div(col, 2), 8)
    y = lax.div(col, 16)
    flip = 1 - core

    def dev(x_, y_, z_, c_):
        return (x_, y_ * 16 + z_ * 2 + c_)

    def mod4(v):
        return lax.rem(v, 4)

    d_sib = dev(x, y, z, flip)
    d_x = [dev(mod4(x + d), y, z, core) for d in range(4)]
    d_y = [dev(x, mod4(y + d), z, core) for d in range(4)]
    zs = [lax.rem(z + d, 8) for d in range(8)]
    d_z = [dev(x, y, zs[d], core) for d in range(8)]
    d_a, d_b = (d_x, d_y) * 2, (d_y, d_x) * 2
    x_at, y_at = [mod4(x + d) for d in range(4)], [mod4(y + d) for d in range(4)]
    ax, bx = (x_at, y_at) * 2, (y_at, x_at) * 2

    loads, sends, pend = [], [], {}

    def load(src, dst):
        cp = pltpu.make_async_copy(src, dst, load_sem.at[len(loads)])
        cp.start()
        loads.append(cp)
        return cp

    starts = [0, 4] + list(range(8, NCH + 1, GRP))
    spans = list(zip(starts[:-1], starts[1:], strict=True))

    def load_span(lo, hi):
        part = pl.ds(lo, hi - lo)
        pairs = ((linv_h, linv), (rhs_h, rhs), (loff_h, loff))
        return [load(src.at[part], dst.at[part]) for src, dst in pairs]

    span_loads = [load_span(*spans[0])]
    po_load = load(po_h, pov)
    span_loads += [load_span(*span) for span in spans[1:]]

    barrier = pltpu.get_barrier_semaphore()
    peers = [d_sib] + d_x[1:] + d_y[1:] + d_z[1:]
    for peer in peers:
        pl.semaphore_signal(barrier, inc=1, device_id=peer, device_id_type=MESH)

    run[NCH] = jnp.zeros((128, 128), F32)

    def table():
        po_load.wait()
        mine = jnp.concatenate(
            [pov[...], jnp.full((1, 128 - NCH), -1, jnp.int32)], axis=1
        )
        rows = jnp.broadcast_to(mine, (128, 128))
        lane = lax.broadcasted_iota(jnp.int32, (128, 128), 1)
        child = lax.broadcasted_iota(jnp.int32, (128, 128), 0)
        label = jnp.where(lane < 64, rows, lane - 64)
        hit = (rows.T == label) & (child < jnp.where(lane < 64, lane, NCH))
        last = jnp.max(jnp.where(hit, child, -1), axis=0, keepdims=True)
        tabv[...] = jnp.where(last < 0, NCH, last)
        cp = pltpu.make_async_copy(tabv, tab, tab_sem.at[0])
        cp.start()
        return cp

    for k, (lo, hi) in enumerate(spans):
        for cp in span_loads[k]:
            cp.wait()
        terms = []
        for c in range(lo, hi):
            f = mm(linv[c], rhs[c]).astype(BF)
            fwd[c] = f
            term = mm_nt(f.T, loff[c])
            if k < 2:
                run[c] = term
            terms.append(term)
        if k == 0:
            tab_copy = table()
        elif k == 1:
            upper_loads = [load(uinv_h, uinv), load(uoff_h, uoff)]
            parent_loads = [
                load(prhs_h, prhs),
                load(plinv_h, plinv),
                load(puinv_h, puinv),
            ]
            tab_copy.wait()
            for c in range(hi):
                run[c] = run[c] + run[tab[0, c]]
        else:
            for c in range(lo, hi):
                run[c] = terms[c - lo] + run[tab[0, c]]

    def mine_of(t, b_, a_, zz, core_):
        x_, y_ = (b_, a_) if t % 2 else (a_, b_)
        row = pl.multiple_of(x_ * 32, 32)
        last_ = tab[0, 64 + y_ * 16 + zs[NEAR[t * 2 + zz]] * 2 + core_]
        return run[last_, pl.ds(row, 32), :]

    def remote(src, dst, slot, dev_):
        return pltpu.make_async_remote_copy(
            src_ref=src,
            dst_ref=dst,
            send_sem=send_sem.at[slot],
            recv_sem=recv_sem.at[slot],
            device_id=dev_,
            device_id_type=MESH,
        )

    def send(src, dst, slot, dev_):
        cp = remote(src, dst, slot, dev_)
        cp.start()
        sends.append(cp)
        pend[slot] = src

    def arrived(dst, slot):
        remote(dst, dst, slot, d_sib).wait_recv()
        pend.pop(slot)

    slots = {}

    def slot(*key):
        return slots.setdefault(key, len(slots))

    order = (2, 1, 3, 0)
    far_first = (3, 2, 1, 0)

    def row_of(b_):
        return pl.ds(b_ * 8, 8)

    waited = False
    for e in order:
        for t in far_first:
            b_ = bx[t][e]
            for a_ in range(4):
                for zz in range(2):
                    v = mine_of(t, b_, a_, zz, flip)
                    sib[t, b_ * 8 + a_ * 2 + zz] = v.astype(BF)
            if not waited:
                pl.semaphore_wait(barrier, len(peers))
                waited = True
            rows_ = row_of(b_)
            send(sib.at[t, rows_], sibr.at[t, rows_], slot("s0", t, e), d_sib)

    for e in order:
        for t in far_first:
            b_ = bx[t][e]
            arrived(sibr.at[t, row_of(b_)], slot("s0", t, e))
            for d in order[:3]:
                a_ = ax[t][d]
                for zz in range(2):
                    u = b_ * 8 + a_ * 2 + zz
                    v = mine_of(t, b_, a_, zz, core) + sibr[t, u].astype(F32)
                    snd[t, u] = v.astype(BF)
                src = snd.at[t, pl.ds(b_ * 8 + a_ * 2, 2)]
                send(src, fin.at[t, d - 1, e], slot("f", t, d, e), d_a[t][d])

    def at_a(t, e, zz):
        b_, a_ = bx[t][e], ax[t][0]
        v = mine_of(t, b_, a_, zz, core) + sibr[t, b_ * 8 + a_ * 2 + zz].astype(F32)
        for d in range(3):
            v = v + fin[t, d, e, zz].astype(F32)
        return v

    for e in order:
        for t in far_first:
            for d in order[:3]:
                arrived(fin.at[t, d - 1, e], slot("f", t, d, e))
            for zz in range(2):
                v = at_a(t, e, zz)
                if e == 0:
                    held[t * 2 + zz] = v
                else:
                    snd2[t, e - 1, zz] = v.astype(BF)
            if e:
                send(snd2.at[t, e - 1], gin.at[t, e - 1], slot("g", t, e), d_b[t][e])

    for t in far_first:
        for e in order[:3]:
            arrived(gin.at[t, e - 1], slot("g", t, e))
        for zz in (1, 0):
            pos = t * 2 + zz
            v = held[pos]
            for e in range(3):
                v = v + gin[t, e, zz].astype(F32)
            if pos == 0:
                total = v
                continue
            d = NEAR[pos]
            zr_out[d - 1] = v.astype(BF)
            send(zr_out.at[d - 1], zr.at[d - 1], slot("z", d), d_z[d])
    held[0] = total

    for cp in parent_loads:
        cp.wait()
    prt[...] = prhs[0].astype(F32).T
    for cp in upper_loads:
        cp.wait()

    def prepare(i):
        for j in range(4):
            c = i * 4 + j
            ui = uinv[c]
            ufwd[c] = mm(ui, fwd[c])
            mat[c] = mm(ui, uoff[c]).astype(BF)

    loop(NCH // 4, prepare)

    total = held[0]
    for d in range(1, 8):
        arrived(zr.at[d - 1], slot("z", d))
        total = total + zr[d - 1].astype(F32)

    res = (prt[pl.ds(pl.multiple_of(x * 32, 32), 32), :] - total).astype(BF)
    pf = mm_nt(res, plinv[0]).astype(BF)

    def unit(pos):
        t = pos // 2
        return (core * 4 + t) * 32 + bx[t][0] * 8 + ax[t][0] * 2 + pos % 2

    sol[...] = mm_nt(pf, puinv[0]).astype(BF)
    gath[unit(0)] = sol[...]

    for d in (4, 3, 5, 2, 6, 1, 7):
        dst = gath.at[unit(NEAR.index(8 - d))]
        send(sol, dst, slot("bz", d), d_z[d])

    def share(ref_slice, slot_, dev_):
        send(gath.at[ref_slice], gath.at[ref_slice], slot_, dev_)

    def piece(t, e, d, core_=core):
        return pl.ds((core_ * 4 + t) * 32 + bx[t][e] * 8 + ax[t][d] * 2, 2)

    def whole_row(t, e, core_=core):
        return pl.ds((core_ * 4 + t) * 32 + bx[t][e] * 8, 8)

    def along_a(t, e):
        for d in order[:3]:
            share(piece(t, e, 0), slot("ba", t, e, d), d_a[t][d])

    def along_b(t):
        for pos in (t * 2, t * 2 + 1):
            if pos:
                arrived(gath.at[unit(pos)], slot("bz", 8 - NEAR[pos]))
        for e in order[:3]:
            share(piece(t, 0, 0), slot("bb", t, e), d_b[t][e])
        along_a(t, 0)

    def along_row(t, e):
        arrived(gath.at[piece(t, e, 0)], slot("bb", t, 4 - e))
        along_a(t, e)

    def across(t, e):
        for d in (1, 3, 2):
            arrived(gath.at[piece(t, e, d)], slot("ba", t, e, 4 - d))
        share(whole_row(t, e), slot("o", t, e), d_sib)

    for t in PARTS:
        along_b(t)
    for t in (0, 1):
        for e in (1, 3, 2):
            along_row(t, e)
    for t in (0, 1):
        across(t, 0)
    for t in (2, 3):
        for e in (1, 3, 2):
            along_row(t, e)
    for t in (0, 1):
        for e in (1, 3, 2):
            across(t, e)
    for e in (0, 1, 3, 2):
        for t in (2, 3):
            across(t, e)
    for t in PARTS:
        for e in (0, 1, 3, 2):
            arrived(gath.at[whole_row(t, e, flip)], slot("o", t, e))
    for cp in sends:
        cp.wait_send()


def backward_kernel(po, gath, ufwd, mat, out_h, psol_h, out, psol, sem):
    col = lax.axis_index("col")
    z = lax.rem(lax.div(col, 2), 8)
    psol[0] = parent_of_units(gath, col, z).T
    copies = []

    def put(src, dst):
        cp = pltpu.make_async_copy(src, dst, sem.at[len(copies)])
        cp.start()
        copies.append(cp)

    put(psol, psol_h)
    for k in range(CHUNKS):
        for c in range(k * GRP, (k + 1) * GRP):
            s = parent_of_units(gath, po[c], z)
            out[c] = (ufwd[c] - mm_nt(mat[c], s)).astype(BF)
        part = pl.ds(k * GRP, GRP)
        put(out.at[part], out_h.at[part])
    for cp in copies:
        cp.wait()


def on_device(
    child_rhs,
    parent_rhs,
    child_lower_inv,
    child_lower_off,
    child_upper_inv,
    child_upper_off,
    parent_lower_inv,
    parent_upper_inv,
    parent_of,
):
    mats = lambda: pltpu.VMEM((NCH, 128, 128), BF)
    one = lambda: pltpu.VMEM((1, 128, 128), BF)
    units = lambda *k: pltpu.VMEM((*k, 32, 128), BF)
    smem = pl.BlockSpec(memory_space=pltpu.SMEM)
    vmem = pl.BlockSpec(memory_space=pltpu.VMEM)
    hbm = pl.BlockSpec(memory_space=pl.ANY)
    gath, ufwd, mat = pl.pallas_call(
        forward_kernel,
        out_shape=(
            jax.ShapeDtypeStruct((256, 32, 128), BF),
            jax.ShapeDtypeStruct((NCH, 128, 128), F32),
            jax.ShapeDtypeStruct((NCH, 128, 128), BF),
        ),
        in_specs=[hbm] * 9,
        out_specs=(vmem, vmem, vmem),
        scratch_shapes=[
            mats(),
            mats(),
            mats(),
            mats(),
            mats(),
            one(),
            one(),
            one(),
            mats(),
            pltpu.VMEM((NCH + 1, 128, 128), F32),
            pltpu.VMEM((1, NCH), jnp.int32),
            pltpu.VMEM((1, 128), jnp.int32),
            pltpu.SMEM((1, 128), jnp.int32),
            units(4, 32),
            units(4, 32),
            units(4, 32),
            units(4, 3, 4, 2),
            units(4, 3, 2),
            units(4, 3, 2),
            pltpu.VMEM((8, 32, 128), F32),
            units(7),
            units(7),
            units(),
            pltpu.VMEM((128, 128), F32),
            pltpu.SemaphoreType.DMA((3 * CHUNKS + 9,)),
            pltpu.SemaphoreType.DMA((1,)),
            pltpu.SemaphoreType.DMA((166,)),
            pltpu.SemaphoreType.DMA((166,)),
        ],
        compiler_params=pltpu.CompilerParams(
            collective_id=0, has_side_effects=True, vmem_limit_bytes=40 * 2**20
        ),
    )(
        *[
            pltpu.with_memory_space_constraint(v, pltpu.HBM)
            for v in (
                parent_of.reshape(1, NCH),
                child_rhs,
                parent_rhs,
                child_lower_inv,
                child_lower_off,
                child_upper_inv,
                child_upper_off,
                parent_lower_inv,
                parent_upper_inv,
            )
        ]
    )
    return pl.pallas_call(
        backward_kernel,
        out_shape=(
            jax.ShapeDtypeStruct(child_rhs.shape, BF),
            jax.ShapeDtypeStruct(parent_rhs.shape, BF),
        ),
        in_specs=[smem, vmem, vmem, vmem],
        out_specs=(hbm, hbm),
        scratch_shapes=[mats(), one(), pltpu.SemaphoreType.DMA((CHUNKS + 1,))],
        compiler_params=pltpu.CompilerParams(vmem_limit_bytes=16 * 2**20),
    )(parent_of, gath, ufwd, mat)


def solution(mesh):
    child = P(("row", "col"), None, None)
    par = P("col", None, None)
    return jax.shard_map(
        on_device,
        mesh=mesh,
        in_specs=(child, par, child, child, child, child, par, par, P(("row", "col"))),
        out_specs=(child, par),
        check_vma=False,
    )
```

```python
import jax
import jax.numpy as jnp
from jax import lax
from jax.experimental import pallas as pl
from jax.experimental.pallas import tpu as pltpu
from jax.sharding import PartitionSpec as P

BF = jnp.bfloat16
F32 = jnp.float32
MESH = pl.DeviceIdType.MESH
NCH = 48
GRP = 8
CHUNKS = NCH // GRP
NT = (((1,), (1,)), ((), ()))


def mm(a, b):
    return jnp.dot(a, b, preferred_element_type=F32)


def mm_nt(a, b):
    return lax.dot_general(a, b, NT, preferred_element_type=F32)


def loop(n, body, unroll=1):
    def step(i, carry):
        body(i)
        return carry

    lax.fori_loop(0, n, step, 0, unroll=unroll)


NEAR = (0, 1, 7, 2, 6, 3, 5, 4)
PARTS = range(4)


def place_of(p, z):
    h, pz, y = lax.rem(p, 2), lax.rem(lax.div(p, 2), 8), lax.div(p, 16)
    far = lax.rem(pz - z + 8, 8)
    pos = jnp.maximum(jnp.minimum(2 * far - 1, 16 - 2 * far), 0)
    t, odd = lax.div(pos, 2), lax.rem(lax.div(pos, 2), 2)
    first = (h * 4 + t) * 32 + lax.rem(pos, 2) + (1 - odd) * y * 8 + odd * y * 2
    return first, (1 - odd) * 2 + odd * 8


def parent_of_units(gath, p, z):
    first, step = place_of(p, z)
    return jnp.concatenate([gath[first + q * step] for q in range(4)], axis=0)


def forward_kernel(
    po_h,
    rhs_h,
    prhs_h,
    linv_h,
    loff_h,
    uinv_h,
    uoff_h,
    plinv_h,
    puinv_h,
    gath,
    ufwd,
    mat,
    rhs,
    linv,
    loff,
    uinv,
    uoff,
    prhs,
    plinv,
    puinv,
    fwd,
    run,
    pov,
    tabv,
    tab,
    sib,
    sibr,
    snd,
    fin,
    snd2,
    gin,
    held,
    zr_out,
    zr,
    sol,
    prt,
    load_sem,
    tab_sem,
    send_sem,
    recv_sem,
):
    x = lax.axis_index("row")
    col = lax.axis_index("col")
    core = lax.rem(col, 2)
    z = lax.rem(lax.div(col, 2), 8)
    y = lax.div(col, 16)
    flip = 1 - core

    def dev(x_, y_, z_, c_):
        return (x_, y_ * 16 + z_ * 2 + c_)

    def mod4(v):
        return lax.rem(v, 4)

    d_sib = dev(x, y, z, flip)
    d_x = [dev(mod4(x + d), y, z, core) for d in range(4)]
    d_y = [dev(x, mod4(y + d), z, core) for d in range(4)]
    zs = [lax.rem(z + d, 8) for d in range(8)]
    d_z = [dev(x, y, zs[d], core) for d in range(8)]
    d_a, d_b = (d_x, d_y) * 2, (d_y, d_x) * 2
    x_at, y_at = [mod4(x + d) for d in range(4)], [mod4(y + d) for d in range(4)]
    ax, bx = (x_at, y_at) * 2, (y_at, x_at) * 2

    loads, sends, pend = [], [], {}

    def load(src, dst):
        cp = pltpu.make_async_copy(src, dst, load_sem.at[len(loads)])
        cp.start()
        loads.append(cp)
        return cp

    starts = [0, 4] + list(range(8, NCH + 1, GRP))
    spans = list(zip(starts[:-1], starts[1:], strict=True))

    def load_span(lo, hi):
        part = pl.ds(lo, hi - lo)
        pairs = ((linv_h, linv), (rhs_h, rhs), (loff_h, loff))
        return [load(src.at[part], dst.at[part]) for src, dst in pairs]

    po_load = load(po_h, pov)
    span_loads = [load_span(*span) for span in spans]
    upper_loads = [load(uinv_h, uinv), load(uoff_h, uoff)]
    parent_loads = [load(prhs_h, prhs), load(plinv_h, plinv), load(puinv_h, puinv)]

    barrier = pltpu.get_barrier_semaphore()
    peers = [d_sib] + d_x[1:] + d_y[1:] + d_z[1:]
    for peer in peers:
        pl.semaphore_signal(barrier, inc=1, device_id=peer, device_id_type=MESH)

    run[NCH] = jnp.zeros((128, 128), F32)

    def table():
        po_load.wait()
        mine = jnp.concatenate(
            [pov[...], jnp.full((1, 128 - NCH), -1, jnp.int32)], axis=1
        )
        rows = jnp.broadcast_to(mine, (128, 128))
        lane = lax.broadcasted_iota(jnp.int32, (128, 128), 1)
        child = lax.broadcasted_iota(jnp.int32, (128, 128), 0)
        label = jnp.where(lane < 64, rows, lane - 64)
        hit = (rows.T == label) & (child < jnp.where(lane < 64, lane, NCH))
        last = jnp.max(jnp.where(hit, child, -1), axis=0, keepdims=True)
        tabv[...] = jnp.where(last < 0, NCH, last)
        cp = pltpu.make_async_copy(tabv, tab, tab_sem.at[0])
        cp.start()
        return cp

    tab_copy = table()
    for k, (lo, hi) in enumerate(spans):
        for cp in span_loads[k]:
            cp.wait()
        terms = []
        for c in range(lo, hi):
            f = mm(linv[c], rhs[c]).astype(BF)
            fwd[c] = f
            term = mm_nt(f.T, loff[c])
            if k < 2:
                run[c] = term
            terms.append(term)
        if k == 1:
            tab_copy.wait()
            for c in range(hi):
                run[c] = run[c] + run[tab[0, c]]
        elif k > 1:
            for c in range(lo, hi):
                run[c] = terms[c - lo] + run[tab[0, c]]

    def mine_of(t, b_, a_, zz, core_):
        x_, y_ = (b_, a_) if t % 2 else (a_, b_)
        row = pl.multiple_of(x_ * 32, 32)
        last_ = tab[0, 64 + y_ * 16 + zs[NEAR[t * 2 + zz]] * 2 + core_]
        return run[last_, pl.ds(row, 32), :]

    def remote(src, dst, slot, dev_):
        return pltpu.make_async_remote_copy(
            src_ref=src,
            dst_ref=dst,
            send_sem=send_sem.at[slot],
            recv_sem=recv_sem.at[slot],
            device_id=dev_,
            device_id_type=MESH,
        )

    def send(src, dst, slot, dev_):
        cp = remote(src, dst, slot, dev_)
        cp.start()
        sends.append(cp)
        pend[slot] = src

    def arrived(dst, slot):
        remote(dst, dst, slot, d_sib).wait_recv()
        pend.pop(slot)

    slots = {}

    def slot(*key):
        return slots.setdefault(key, len(slots))

    order = (2, 1, 3, 0)
    far_first = (3, 2, 1, 0)

    def row_of(b_):
        return pl.ds(b_ * 8, 8)

    waited = False
    for e in order:
        for t in far_first:
            b_ = bx[t][e]
            for a_ in range(4):
                for zz in range(2):
                    v = mine_of(t, b_, a_, zz, flip)
                    sib[t, b_ * 8 + a_ * 2 + zz] = v.astype(BF)
            if not waited:
                pl.semaphore_wait(barrier, len(peers))
                waited = True
            rows_ = row_of(b_)
            send(sib.at[t, rows_], sibr.at[t, rows_], slot("s0", t, e), d_sib)

    for e in order:
        for t in far_first:
            b_ = bx[t][e]
            arrived(sibr.at[t, row_of(b_)], slot("s0", t, e))
            for d in order[:3]:
                a_ = ax[t][d]
                for zz in range(2):
                    u = b_ * 8 + a_ * 2 + zz
                    v = mine_of(t, b_, a_, zz, core) + sibr[t, u].astype(F32)
                    snd[t, u] = v.astype(BF)
                src = snd.at[t, pl.ds(b_ * 8 + a_ * 2, 2)]
                send(src, fin.at[t, d - 1, e], slot("f", t, d, e), d_a[t][d])

    def at_a(t, e, zz):
        b_, a_ = bx[t][e], ax[t][0]
        v = mine_of(t, b_, a_, zz, core) + sibr[t, b_ * 8 + a_ * 2 + zz].astype(F32)
        for d in range(3):
            v = v + fin[t, d, e, zz].astype(F32)
        return v

    for e in order:
        for t in far_first:
            for d in order[:3]:
                arrived(fin.at[t, d - 1, e], slot("f", t, d, e))
            for zz in range(2):
                v = at_a(t, e, zz)
                if e == 0:
                    held[t * 2 + zz] = v
                else:
                    snd2[t, e - 1, zz] = v.astype(BF)
            if e:
                send(snd2.at[t, e - 1], gin.at[t, e - 1], slot("g", t, e), d_b[t][e])

    for t in far_first:
        for e in order[:3]:
            arrived(gin.at[t, e - 1], slot("g", t, e))
        for zz in (1, 0):
            pos = t * 2 + zz
            v = held[pos]
            for e in range(3):
                v = v + gin[t, e, zz].astype(F32)
            if pos == 0:
                total = v
                continue
            d = NEAR[pos]
            zr_out[d - 1] = v.astype(BF)
            send(zr_out.at[d - 1], zr.at[d - 1], slot("z", d), d_z[d])
    held[0] = total

    for cp in parent_loads:
        cp.wait()
    prt[...] = prhs[0].astype(F32).T
    for cp in upper_loads:
        cp.wait()

    def prepare(i):
        for j in range(4):
            c = i * 4 + j
            ui = uinv[c]
            ufwd[c] = mm(ui, fwd[c])
            mat[c] = mm(ui, uoff[c]).astype(BF)

    loop(NCH // 4, prepare)

    total = held[0]
    for d in range(1, 8):
        arrived(zr.at[d - 1], slot("z", d))
        total = total + zr[d - 1].astype(F32)

    res = (prt[pl.ds(pl.multiple_of(x * 32, 32), 32), :] - total).astype(BF)
    pf = mm_nt(res, plinv[0]).astype(BF)

    def unit(pos):
        t = pos // 2
        return (core * 4 + t) * 32 + bx[t][0] * 8 + ax[t][0] * 2 + pos % 2

    sol[...] = mm_nt(pf, puinv[0]).astype(BF)
    gath[unit(0)] = sol[...]

    for d in (4, 3, 5, 2, 6, 1, 7):
        dst = gath.at[unit(NEAR.index(8 - d))]
        send(sol, dst, slot("bz", d), d_z[d])

    def share(ref_slice, slot_, dev_):
        send(gath.at[ref_slice], gath.at[ref_slice], slot_, dev_)

    def piece(t, e, d, core_=core):
        return pl.ds((core_ * 4 + t) * 32 + bx[t][e] * 8 + ax[t][d] * 2, 2)

    def whole_row(t, e, core_=core):
        return pl.ds((core_ * 4 + t) * 32 + bx[t][e] * 8, 8)

    def along_a(t, e):
        for d in order[:3]:
            share(piece(t, e, 0), slot("ba", t, e, d), d_a[t][d])

    def along_b(t):
        for pos in (t * 2, t * 2 + 1):
            if pos:
                arrived(gath.at[unit(pos)], slot("bz", 8 - NEAR[pos]))
        for e in order[:3]:
            share(piece(t, 0, 0), slot("bb", t, e), d_b[t][e])
        along_a(t, 0)

    def along_row(t, e):
        arrived(gath.at[piece(t, e, 0)], slot("bb", t, 4 - e))
        along_a(t, e)

    def across(t, e):
        for d in (1, 3, 2):
            arrived(gath.at[piece(t, e, d)], slot("ba", t, e, 4 - d))
        share(whole_row(t, e), slot("o", t, e), d_sib)

    for t in PARTS:
        along_b(t)
    for t in (0, 1):
        for e in (1, 3, 2):
            along_row(t, e)
    for t in (0, 1):
        across(t, 0)
    for t in (2, 3):
        for e in (1, 3, 2):
            along_row(t, e)
    for t in (0, 1):
        for e in (1, 3, 2):
            across(t, e)
    for e in (0, 1, 3, 2):
        for t in (2, 3):
            across(t, e)
    for t in PARTS:
        for e in (0, 1, 3, 2):
            arrived(gath.at[whole_row(t, e, flip)], slot("o", t, e))
    for cp in sends:
        cp.wait_send()


def backward_kernel(po, gath, ufwd, mat, out_h, psol_h, out, psol, sem):
    col = lax.axis_index("col")
    z = lax.rem(lax.div(col, 2), 8)
    psol[0] = parent_of_units(gath, col, z).T
    copies = []

    def put(src, dst):
        cp = pltpu.make_async_copy(src, dst, sem.at[len(copies)])
        cp.start()
        copies.append(cp)

    put(psol, psol_h)
    for k in range(CHUNKS):
        for c in range(k * GRP, (k + 1) * GRP):
            s = parent_of_units(gath, po[c], z)
            out[c] = (ufwd[c] - mm_nt(mat[c], s)).astype(BF)
        part = pl.ds(k * GRP, GRP)
        put(out.at[part], out_h.at[part])
    for cp in copies:
        cp.wait()


def on_device(
    child_rhs,
    parent_rhs,
    child_lower_inv,
    child_lower_off,
    child_upper_inv,
    child_upper_off,
    parent_lower_inv,
    parent_upper_inv,
    parent_of,
):
    mats = lambda: pltpu.VMEM((NCH, 128, 128), BF)
    one = lambda: pltpu.VMEM((1, 128, 128), BF)
    units = lambda *k: pltpu.VMEM((*k, 32, 128), BF)
    smem = pl.BlockSpec(memory_space=pltpu.SMEM)
    vmem = pl.BlockSpec(memory_space=pltpu.VMEM)
    hbm = pl.BlockSpec(memory_space=pl.ANY)
    gath, ufwd, mat = pl.pallas_call(
        forward_kernel,
        out_shape=(
            jax.ShapeDtypeStruct((256, 32, 128), BF),
            jax.ShapeDtypeStruct((NCH, 128, 128), F32),
            jax.ShapeDtypeStruct((NCH, 128, 128), BF),
        ),
        in_specs=[hbm] * 9,
        out_specs=(vmem, vmem, vmem),
        scratch_shapes=[
            mats(),
            mats(),
            mats(),
            mats(),
            mats(),
            one(),
            one(),
            one(),
            mats(),
            pltpu.VMEM((NCH + 1, 128, 128), F32),
            pltpu.VMEM((1, NCH), jnp.int32),
            pltpu.VMEM((1, 128), jnp.int32),
            pltpu.SMEM((1, 128), jnp.int32),
            units(4, 32),
            units(4, 32),
            units(4, 32),
            units(4, 3, 4, 2),
            units(4, 3, 2),
            units(4, 3, 2),
            pltpu.VMEM((8, 32, 128), F32),
            units(7),
            units(7),
            units(),
            pltpu.VMEM((128, 128), F32),
            pltpu.SemaphoreType.DMA((3 * CHUNKS + 9,)),
            pltpu.SemaphoreType.DMA((1,)),
            pltpu.SemaphoreType.DMA((166,)),
            pltpu.SemaphoreType.DMA((166,)),
        ],
        compiler_params=pltpu.CompilerParams(
            collective_id=0, has_side_effects=True, vmem_limit_bytes=40 * 2**20
        ),
    )(
        *[
            pltpu.with_memory_space_constraint(v, pltpu.HBM)
            for v in (
                parent_of.reshape(1, NCH),
                child_rhs,
                parent_rhs,
                child_lower_inv,
                child_lower_off,
                child_upper_inv,
                child_upper_off,
                parent_lower_inv,
                parent_upper_inv,
            )
        ]
    )
    return pl.pallas_call(
        backward_kernel,
        out_shape=(
            jax.ShapeDtypeStruct(child_rhs.shape, BF),
            jax.ShapeDtypeStruct(parent_rhs.shape, BF),
        ),
        in_specs=[smem, vmem, vmem, vmem],
        out_specs=(hbm, hbm),
        scratch_shapes=[mats(), one(), pltpu.SemaphoreType.DMA((CHUNKS + 1,))],
        compiler_params=pltpu.CompilerParams(vmem_limit_bytes=16 * 2**20),
    )(parent_of, gath, ufwd, mat)


def solution(mesh):
    child = P(("row", "col"), None, None)
    par = P("col", None, None)
    return jax.shard_map(
        on_device,
        mesh=mesh,
        in_specs=(child, par, child, child, child, child, par, par, P(("row", "col"))),
        out_specs=(child, par),
        check_vma=False,
    )
```

```python
import jax
import jax.numpy as jnp
from jax import lax
from jax.experimental import pallas as pl
from jax.experimental.pallas import tpu as pltpu
from jax.sharding import PartitionSpec as P

BF = jnp.bfloat16
F32 = jnp.float32
MESH = pl.DeviceIdType.MESH
NCH = 48
GRP = 8
CHUNKS = NCH // GRP
NT = (((1,), (1,)), ((), ()))


def mm(a, b):
    return jnp.dot(a, b, preferred_element_type=F32)


def mm_nt(a, b):
    return lax.dot_general(a, b, NT, preferred_element_type=F32)


def loop(n, body, unroll=1):
    def step(i, carry):
        body(i)
        return carry

    lax.fori_loop(0, n, step, 0, unroll=unroll)


NEAR = (0, 1, 7, 2, 6, 3, 5, 4)
PARTS = range(4)


def place_of(p, z):
    h, pz, y = lax.rem(p, 2), lax.rem(lax.div(p, 2), 8), lax.div(p, 16)
    far = lax.rem(pz - z + 8, 8)
    pos = jnp.maximum(jnp.minimum(2 * far - 1, 16 - 2 * far), 0)
    t, odd = lax.div(pos, 2), lax.rem(lax.div(pos, 2), 2)
    first = (h * 4 + t) * 32 + lax.rem(pos, 2) + (1 - odd) * y * 8 + odd * y * 2
    return first, (1 - odd) * 2 + odd * 8


def parent_of_units(gath, p, z):
    first, step = place_of(p, z)
    return jnp.concatenate([gath[first + q * step] for q in range(4)], axis=0)


def forward_kernel(
    po_h,
    rhs_h,
    prhs_h,
    linv_h,
    loff_h,
    uinv_h,
    uoff_h,
    plinv_h,
    puinv_h,
    gath,
    ufwd,
    mat,
    rhs,
    linv,
    loff,
    uinv,
    uoff,
    prhs,
    plinv,
    puinv,
    fwd,
    run,
    pov,
    tabv,
    tab,
    sib,
    sibr,
    snd,
    fin,
    snd2,
    gin,
    held,
    zr_out,
    zr,
    sol,
    prt,
    load_sem,
    tab_sem,
    send_sem,
    recv_sem,
):
    x = lax.axis_index("row")
    col = lax.axis_index("col")
    core = lax.rem(col, 2)
    z = lax.rem(lax.div(col, 2), 8)
    y = lax.div(col, 16)
    flip = 1 - core

    def dev(x_, y_, z_, c_):
        return (x_, y_ * 16 + z_ * 2 + c_)

    def mod4(v):
        return lax.rem(v, 4)

    d_sib = dev(x, y, z, flip)
    d_x = [dev(mod4(x + d), y, z, core) for d in range(4)]
    d_y = [dev(x, mod4(y + d), z, core) for d in range(4)]
    zs = [lax.rem(z + d, 8) for d in range(8)]
    d_z = [dev(x, y, zs[d], core) for d in range(8)]
    d_a, d_b = (d_x, d_y) * 2, (d_y, d_x) * 2
    x_at, y_at = [mod4(x + d) for d in range(4)], [mod4(y + d) for d in range(4)]
    ax, bx = (x_at, y_at) * 2, (y_at, x_at) * 2

    loads, sends, pend = [], [], {}

    def load(src, dst):
        cp = pltpu.make_async_copy(src, dst, load_sem.at[len(loads)])
        cp.start()
        loads.append(cp)
        return cp

    starts = [0, 4] + list(range(8, NCH + 1, GRP))
    spans = list(zip(starts[:-1], starts[1:], strict=True))

    def load_span(lo, hi):
        part = pl.ds(lo, hi - lo)
        pairs = ((linv_h, linv), (rhs_h, rhs), (loff_h, loff))
        return [load(src.at[part], dst.at[part]) for src, dst in pairs]

    po_load = load(po_h, pov)
    span_loads = [load_span(*span) for span in spans]
    upper_loads = [load(uinv_h, uinv), load(uoff_h, uoff)]
    parent_loads = [load(prhs_h, prhs), load(plinv_h, plinv), load(puinv_h, puinv)]

    barrier = pltpu.get_barrier_semaphore()
    peers = [d_sib] + d_x[1:] + d_y[1:] + d_z[1:]
    for peer in peers:
        pl.semaphore_signal(barrier, inc=1, device_id=peer, device_id_type=MESH)

    run[NCH] = jnp.zeros((128, 128), F32)

    def table():
        po_load.wait()
        mine = jnp.concatenate(
            [pov[...], jnp.full((1, 128 - NCH), -1, jnp.int32)], axis=1
        )
        rows = jnp.broadcast_to(mine, (128, 128))
        lane = lax.broadcasted_iota(jnp.int32, (128, 128), 1)
        child = lax.broadcasted_iota(jnp.int32, (128, 128), 0)
        label = jnp.where(lane < 64, rows, lane - 64)
        hit = (rows.T == label) & (child < jnp.where(lane < 64, lane, NCH))
        last = jnp.max(jnp.where(hit, child, -1), axis=0, keepdims=True)
        tabv[...] = jnp.where(last < 0, NCH, last)
        cp = pltpu.make_async_copy(tabv, tab, tab_sem.at[0])
        cp.start()
        return cp

    tab_copy = table()
    for k, (lo, hi) in enumerate(spans):
        for cp in span_loads[k]:
            cp.wait()
        terms = []
        for c in range(lo, hi):
            f = mm(linv[c], rhs[c]).astype(BF)
            fwd[c] = f
            term = mm_nt(f.T, loff[c])
            if k < 2:
                run[c] = term
            terms.append(term)
        if k == 1:
            tab_copy.wait()
            for c in range(hi):
                run[c] = run[c] + run[tab[0, c]]
        elif k > 1:
            for c in range(lo, hi):
                run[c] = terms[c - lo] + run[tab[0, c]]

    def mine_of(t, b_, a_, zz, core_):
        x_, y_ = (b_, a_) if t % 2 else (a_, b_)
        row = pl.multiple_of(x_ * 32, 32)
        last_ = tab[0, 64 + y_ * 16 + zs[NEAR[t * 2 + zz]] * 2 + core_]
        return run[last_, pl.ds(row, 32), :]

    def remote(src, dst, slot, dev_):
        return pltpu.make_async_remote_copy(
            src_ref=src,
            dst_ref=dst,
            send_sem=send_sem.at[slot],
            recv_sem=recv_sem.at[slot],
            device_id=dev_,
            device_id_type=MESH,
        )

    def send(src, dst, slot, dev_):
        cp = remote(src, dst, slot, dev_)
        cp.start()
        sends.append(cp)
        pend[slot] = src

    def arrived(dst, slot):
        remote(dst, dst, slot, d_sib).wait_recv()
        pend.pop(slot)

    slots = {}

    def slot(*key):
        return slots.setdefault(key, len(slots))

    order = (2, 1, 3, 0)
    far_first = (3, 2, 1, 0)
    rows_first = [(t, e) for ts in ((3, 2), (1, 0)) for e in order[:3] for t in ts]
    rows_first += [(t, 0) for t in far_first]

    def row_of(b_):
        return pl.ds(b_ * 8, 8)

    waited = False
    for t, e in rows_first:
        b_ = bx[t][e]
        for a_ in range(4):
            for zz in range(2):
                v = mine_of(t, b_, a_, zz, flip)
                sib[t, b_ * 8 + a_ * 2 + zz] = v.astype(BF)
        if not waited:
            pl.semaphore_wait(barrier, len(peers))
            waited = True
        rows_ = row_of(b_)
        send(sib.at[t, rows_], sibr.at[t, rows_], slot("s0", t, e), d_sib)

    for t, e in rows_first:
        b_ = bx[t][e]
        arrived(sibr.at[t, row_of(b_)], slot("s0", t, e))
        for d in order[:3]:
            a_ = ax[t][d]
            for zz in range(2):
                u = b_ * 8 + a_ * 2 + zz
                v = mine_of(t, b_, a_, zz, core) + sibr[t, u].astype(F32)
                snd[t, u] = v.astype(BF)
            src = snd.at[t, pl.ds(b_ * 8 + a_ * 2, 2)]
            send(src, fin.at[t, d - 1, e], slot("f", t, d, e), d_a[t][d])

    def at_a(t, e, zz):
        b_, a_ = bx[t][e], ax[t][0]
        v = mine_of(t, b_, a_, zz, core) + sibr[t, b_ * 8 + a_ * 2 + zz].astype(F32)
        for d in range(3):
            v = v + fin[t, d, e, zz].astype(F32)
        return v

    for t, e in rows_first:
        for d in order[:3]:
            arrived(fin.at[t, d - 1, e], slot("f", t, d, e))
        for zz in range(2):
            v = at_a(t, e, zz)
            if e == 0:
                held[t * 2 + zz] = v
            else:
                snd2[t, e - 1, zz] = v.astype(BF)
        if e:
            send(snd2.at[t, e - 1], gin.at[t, e - 1], slot("g", t, e), d_b[t][e])

    for t in far_first:
        for e in order[:3]:
            arrived(gin.at[t, e - 1], slot("g", t, e))
        for zz in (1, 0):
            pos = t * 2 + zz
            v = held[pos]
            for e in range(3):
                v = v + gin[t, e, zz].astype(F32)
            if pos == 0:
                total = v
                continue
            d = NEAR[pos]
            zr_out[d - 1] = v.astype(BF)
            send(zr_out.at[d - 1], zr.at[d - 1], slot("z", d), d_z[d])
    held[0] = total

    for cp in parent_loads:
        cp.wait()
    prt[...] = prhs[0].astype(F32).T
    for cp in upper_loads:
        cp.wait()

    def prepare(i):
        for j in range(4):
            c = i * 4 + j
            ui = uinv[c]
            ufwd[c] = mm(ui, fwd[c])
            mat[c] = mm(ui, uoff[c]).astype(BF)

    loop(NCH // 4, prepare)

    total = held[0]
    for d in range(1, 8):
        arrived(zr.at[d - 1], slot("z", d))
        total = total + zr[d - 1].astype(F32)

    res = (prt[pl.ds(pl.multiple_of(x * 32, 32), 32), :] - total).astype(BF)
    pf = mm_nt(res, plinv[0]).astype(BF)

    def unit(pos):
        t = pos // 2
        return (core * 4 + t) * 32 + bx[t][0] * 8 + ax[t][0] * 2 + pos % 2

    sol[...] = mm_nt(pf, puinv[0]).astype(BF)
    gath[unit(0)] = sol[...]

    for d in (4, 3, 5, 2, 6, 1, 7):
        dst = gath.at[unit(NEAR.index(8 - d))]
        send(sol, dst, slot("bz", d), d_z[d])

    def share(ref_slice, slot_, dev_):
        send(gath.at[ref_slice], gath.at[ref_slice], slot_, dev_)

    def piece(t, e, d, core_=core):
        return pl.ds((core_ * 4 + t) * 32 + bx[t][e] * 8 + ax[t][d] * 2, 2)

    def whole_row(t, e, core_=core):
        return pl.ds((core_ * 4 + t) * 32 + bx[t][e] * 8, 8)

    def along_a(t, e):
        for d in order[:3]:
            share(piece(t, e, 0), slot("ba", t, e, d), d_a[t][d])

    def along_b(t):
        for pos in (t * 2, t * 2 + 1):
            if pos:
                arrived(gath.at[unit(pos)], slot("bz", 8 - NEAR[pos]))
        for e in order[:3]:
            share(piece(t, 0, 0), slot("bb", t, e), d_b[t][e])
        along_a(t, 0)

    def along_row(t, e):
        arrived(gath.at[piece(t, e, 0)], slot("bb", t, 4 - e))
        along_a(t, e)

    def across(t, e):
        for d in (1, 3, 2):
            arrived(gath.at[piece(t, e, d)], slot("ba", t, e, 4 - d))
        share(whole_row(t, e), slot("o", t, e), d_sib)

    for t in PARTS:
        along_b(t)
    for t in (0, 1):
        for e in (1, 3, 2):
            along_row(t, e)
    for t in (0, 1):
        across(t, 0)
    for t in (2, 3):
        for e in (1, 3, 2):
            along_row(t, e)
    for t in (0, 1):
        for e in (1, 3, 2):
            across(t, e)
    for e in (0, 1, 3, 2):
        for t in (2, 3):
            across(t, e)
    for t in PARTS:
        for e in (0, 1, 3, 2):
            arrived(gath.at[whole_row(t, e, flip)], slot("o", t, e))
    for cp in sends:
        cp.wait_send()


def backward_kernel(po, gath, ufwd, mat, out_h, psol_h, out, psol, sem):
    col = lax.axis_index("col")
    z = lax.rem(lax.div(col, 2), 8)
    psol[0] = parent_of_units(gath, col, z).T
    copies = []

    def put(src, dst):
        cp = pltpu.make_async_copy(src, dst, sem.at[len(copies)])
        cp.start()
        copies.append(cp)

    put(psol, psol_h)
    for k in range(CHUNKS):
        for c in range(k * GRP, (k + 1) * GRP):
            s = parent_of_units(gath, po[c], z)
            out[c] = (ufwd[c] - mm_nt(mat[c], s)).astype(BF)
        part = pl.ds(k * GRP, GRP)
        put(out.at[part], out_h.at[part])
    for cp in copies:
        cp.wait()


def on_device(
    child_rhs,
    parent_rhs,
    child_lower_inv,
    child_lower_off,
    child_upper_inv,
    child_upper_off,
    parent_lower_inv,
    parent_upper_inv,
    parent_of,
):
    mats = lambda: pltpu.VMEM((NCH, 128, 128), BF)
    one = lambda: pltpu.VMEM((1, 128, 128), BF)
    units = lambda *k: pltpu.VMEM((*k, 32, 128), BF)
    smem = pl.BlockSpec(memory_space=pltpu.SMEM)
    vmem = pl.BlockSpec(memory_space=pltpu.VMEM)
    hbm = pl.BlockSpec(memory_space=pl.ANY)
    gath, ufwd, mat = pl.pallas_call(
        forward_kernel,
        out_shape=(
            jax.ShapeDtypeStruct((256, 32, 128), BF),
            jax.ShapeDtypeStruct((NCH, 128, 128), F32),
            jax.ShapeDtypeStruct((NCH, 128, 128), BF),
        ),
        in_specs=[hbm] * 9,
        out_specs=(vmem, vmem, vmem),
        scratch_shapes=[
            mats(),
            mats(),
            mats(),
            mats(),
            mats(),
            one(),
            one(),
            one(),
            mats(),
            pltpu.VMEM((NCH + 1, 128, 128), F32),
            pltpu.VMEM((1, NCH), jnp.int32),
            pltpu.VMEM((1, 128), jnp.int32),
            pltpu.SMEM((1, 128), jnp.int32),
            units(4, 32),
            units(4, 32),
            units(4, 32),
            units(4, 3, 4, 2),
            units(4, 3, 2),
            units(4, 3, 2),
            pltpu.VMEM((8, 32, 128), F32),
            units(7),
            units(7),
            units(),
            pltpu.VMEM((128, 128), F32),
            pltpu.SemaphoreType.DMA((3 * CHUNKS + 9,)),
            pltpu.SemaphoreType.DMA((1,)),
            pltpu.SemaphoreType.DMA((166,)),
            pltpu.SemaphoreType.DMA((166,)),
        ],
        compiler_params=pltpu.CompilerParams(
            collective_id=0, has_side_effects=True, vmem_limit_bytes=40 * 2**20
        ),
    )(
        *[
            pltpu.with_memory_space_constraint(v, pltpu.HBM)
            for v in (
                parent_of.reshape(1, NCH),
                child_rhs,
                parent_rhs,
                child_lower_inv,
                child_lower_off,
                child_upper_inv,
                child_upper_off,
                parent_lower_inv,
                parent_upper_inv,
            )
        ]
    )
    return pl.pallas_call(
        backward_kernel,
        out_shape=(
            jax.ShapeDtypeStruct(child_rhs.shape, BF),
            jax.ShapeDtypeStruct(parent_rhs.shape, BF),
        ),
        in_specs=[smem, vmem, vmem, vmem],
        out_specs=(hbm, hbm),
        scratch_shapes=[mats(), one(), pltpu.SemaphoreType.DMA((CHUNKS + 1,))],
        compiler_params=pltpu.CompilerParams(vmem_limit_bytes=16 * 2**20),
    )(parent_of, gath, ufwd, mat)


def solution(mesh):
    child = P(("row", "col"), None, None)
    par = P("col", None, None)
    return jax.shard_map(
        on_device,
        mesh=mesh,
        in_specs=(child, par, child, child, child, child, par, par, P(("row", "col"))),
        out_specs=(child, par),
        check_vma=False,
    )
```

```python
import jax
import jax.numpy as jnp
from jax import lax
from jax.experimental import pallas as pl
from jax.experimental.pallas import tpu as pltpu
from jax.sharding import PartitionSpec as P

BF = jnp.bfloat16
F32 = jnp.float32
MESH = pl.DeviceIdType.MESH
NCH = 48
GRP = 8
CHUNKS = NCH // GRP
NT = (((1,), (1,)), ((), ()))


def mm(a, b):
    return jnp.dot(a, b, preferred_element_type=F32)


def mm_nt(a, b):
    return lax.dot_general(a, b, NT, preferred_element_type=F32)


def loop(n, body, unroll=1):
    def step(i, carry):
        body(i)
        return carry

    lax.fori_loop(0, n, step, 0, unroll=unroll)


NEAR = (0, 1, 7, 2, 6, 3, 5, 4)
PARTS = range(4)


def place_of(p, z):
    h, pz, y = lax.rem(p, 2), lax.rem(lax.div(p, 2), 8), lax.div(p, 16)
    far = lax.rem(pz - z + 8, 8)
    pos = jnp.maximum(jnp.minimum(2 * far - 1, 16 - 2 * far), 0)
    t, odd = lax.div(pos, 2), lax.rem(lax.div(pos, 2), 2)
    first = (h * 4 + t) * 32 + lax.rem(pos, 2) + (1 - odd) * y * 8 + odd * y * 2
    return first, (1 - odd) * 2 + odd * 8


def parent_of_units(gath, p, z):
    first, step = place_of(p, z)
    return jnp.concatenate([gath[first + q * step] for q in range(4)], axis=0)


def forward_kernel(
    po_h,
    rhs_h,
    prhs_h,
    linv_h,
    loff_h,
    uinv_h,
    uoff_h,
    plinv_h,
    puinv_h,
    gath,
    ufwd,
    mat,
    rhs,
    linv,
    loff,
    uinv,
    uoff,
    prhs,
    plinv,
    puinv,
    fwd,
    run,
    pov,
    tabv,
    tab,
    sib,
    sibr,
    snd,
    fin,
    snd2,
    gin,
    held,
    zr_out,
    zr,
    sol,
    prt,
    load_sem,
    tab_sem,
    send_sem,
    recv_sem,
):
    x = lax.axis_index("row")
    col = lax.axis_index("col")
    core = lax.rem(col, 2)
    z = lax.rem(lax.div(col, 2), 8)
    y = lax.div(col, 16)
    flip = 1 - core

    def dev(x_, y_, z_, c_):
        return (x_, y_ * 16 + z_ * 2 + c_)

    def mod4(v):
        return lax.rem(v, 4)

    d_sib = dev(x, y, z, flip)
    d_x = [dev(mod4(x + d), y, z, core) for d in range(4)]
    d_y = [dev(x, mod4(y + d), z, core) for d in range(4)]
    zs = [lax.rem(z + d, 8) for d in range(8)]
    d_z = [dev(x, y, zs[d], core) for d in range(8)]
    d_a, d_b = (d_x, d_y) * 2, (d_y, d_x) * 2
    x_at, y_at = [mod4(x + d) for d in range(4)], [mod4(y + d) for d in range(4)]
    ax, bx = (x_at, y_at) * 2, (y_at, x_at) * 2

    loads = []

    def load(src, dst):
        cp = pltpu.make_async_copy(src, dst, load_sem.at[len(loads)])
        cp.start()
        loads.append(cp)
        return cp

    starts = [0, 4] + list(range(8, NCH + 1, GRP))
    spans = list(zip(starts[:-1], starts[1:], strict=True))

    def load_span(lo, hi):
        part = pl.ds(lo, hi - lo)
        pairs = ((linv_h, linv), (rhs_h, rhs), (loff_h, loff))
        return [load(src.at[part], dst.at[part]) for src, dst in pairs]

    po_load = load(po_h, pov)
    span_loads = [load_span(*span) for span in spans]
    upper_loads = [load(uinv_h, uinv), load(uoff_h, uoff)]
    parent_loads = [load(prhs_h, prhs), load(plinv_h, plinv), load(puinv_h, puinv)]

    barrier = pltpu.get_barrier_semaphore()
    peers = [d_sib] + d_x[1:] + d_y[1:] + d_z[1:]
    for peer in peers:
        pl.semaphore_signal(barrier, inc=1, device_id=peer, device_id_type=MESH)

    run[NCH] = jnp.zeros((128, 128), F32)

    def table():
        po_load.wait()
        mine = jnp.concatenate(
            [pov[...], jnp.full((1, 128 - NCH), -1, jnp.int32)], axis=1
        )
        rows = jnp.broadcast_to(mine, (128, 128))
        lane = lax.broadcasted_iota(jnp.int32, (128, 128), 1)
        child = lax.broadcasted_iota(jnp.int32, (128, 128), 0)
        label = jnp.where(lane < 64, rows, lane - 64)
        hit = (rows.T == label) & (child < jnp.where(lane < 64, lane, NCH))
        last = jnp.max(jnp.where(hit, child, -1), axis=0, keepdims=True)
        tabv[...] = jnp.where(last < 0, NCH, last)
        cp = pltpu.make_async_copy(tabv, tab, tab_sem.at[0])
        cp.start()
        return cp

    tab_copy = table()
    for k, (lo, hi) in enumerate(spans):
        for cp in span_loads[k]:
            cp.wait()
        terms = []
        for c in range(lo, hi):
            f = mm(linv[c], rhs[c]).astype(BF)
            fwd[c] = f
            term = mm_nt(f.T, loff[c])
            if k < 2:
                run[c] = term
            terms.append(term)
        if k == 1:
            tab_copy.wait()
            for c in range(hi):
                run[c] = run[c] + run[tab[0, c]]
        elif k > 1:
            for c in range(lo, hi):
                run[c] = terms[c - lo] + run[tab[0, c]]

    def mine_of(t, b_, a_, zz, core_):
        x_, y_ = (b_, a_) if t % 2 else (a_, b_)
        row = pl.multiple_of(x_ * 32, 32)
        last_ = tab[0, 64 + y_ * 16 + zs[NEAR[t * 2 + zz]] * 2 + core_]
        return run[last_, pl.ds(row, 32), :]

    stages = ("s0", "f", "g", "z", "bz", "bb", "ba", "o")
    slots = {}

    def slot(*key):
        return slots.setdefault(key, len(slots))

    def remote(src, dst, sent, got, dev_):
        return pltpu.make_async_remote_copy(
            src_ref=src,
            dst_ref=dst,
            send_sem=send_sem.at[sent],
            recv_sem=recv_sem.at[got],
            device_id=dev_,
            device_id_type=MESH,
        )

    def send(src, dst, dev_, stage, *key):
        remote(src, dst, stages.index(stage), slot(stage, *key), dev_).start()

    def arrived(dst, *key):
        remote(dst, dst, 0, slot(*key), d_sib).wait_recv()

    order = (2, 1, 3, 0)
    far_first = (3, 2, 1, 0)
    rows_first = [(t, e) for ts in ((3, 2), (1, 0)) for e in order[:3] for t in ts]
    rows_first += [(t, 0) for t in far_first]

    def row_of(b_):
        return pl.ds(b_ * 8, 8)

    waited = False
    for t, e in rows_first:
        b_ = bx[t][e]
        for a_ in range(4):
            for zz in range(2):
                v = mine_of(t, b_, a_, zz, flip)
                sib[t, b_ * 8 + a_ * 2 + zz] = v.astype(BF)
        if not waited:
            pl.semaphore_wait(barrier, len(peers))
            waited = True
        rows_ = row_of(b_)
        send(sib.at[t, rows_], sibr.at[t, rows_], d_sib, "s0", t, e)

    for t, e in rows_first:
        b_ = bx[t][e]
        arrived(sibr.at[t, row_of(b_)], "s0", t, e)
        for d in order[:3]:
            a_ = ax[t][d]
            for zz in range(2):
                u = b_ * 8 + a_ * 2 + zz
                v = mine_of(t, b_, a_, zz, core) + sibr[t, u].astype(F32)
                snd[t, u] = v.astype(BF)
            src = snd.at[t, pl.ds(b_ * 8 + a_ * 2, 2)]
            send(src, fin.at[t, e, d - 1], d_a[t][d], "f", t, e)

    def at_a(t, e, zz):
        b_, a_ = bx[t][e], ax[t][0]
        v = mine_of(t, b_, a_, zz, core) + sibr[t, b_ * 8 + a_ * 2 + zz].astype(F32)
        for d in range(3):
            v = v + fin[t, e, d, zz].astype(F32)
        return v

    for t, e in rows_first:
        arrived(fin.at[t, e], "f", t, e)
        for zz in range(2):
            v = at_a(t, e, zz)
            if e == 0:
                held[t * 2 + zz] = v
            else:
                snd2[t, e - 1, zz] = v.astype(BF)
        if e:
            send(snd2.at[t, e - 1], gin.at[t, e - 1], d_b[t][e], "g", t)

    for t in far_first:
        arrived(gin.at[t], "g", t)
        for zz in (1, 0):
            pos = t * 2 + zz
            v = held[pos]
            for e in range(3):
                v = v + gin[t, e, zz].astype(F32)
            if pos == 0:
                total = v
                continue
            d = NEAR[pos]
            zr_out[d - 1] = v.astype(BF)
            send(zr_out.at[d - 1], zr.at[d - 1], d_z[d], "z")
    held[0] = total

    for cp in parent_loads:
        cp.wait()
    prt[...] = prhs[0].astype(F32).T
    for cp in upper_loads:
        cp.wait()

    def prepare(i):
        for j in range(4):
            c = i * 4 + j
            ui = uinv[c]
            ufwd[c] = mm(ui, fwd[c])
            mat[c] = mm(ui, uoff[c]).astype(BF)

    loop(NCH // 4, prepare)

    total = held[0]
    arrived(zr, "z")
    for d in range(1, 8):
        total = total + zr[d - 1].astype(F32)

    res = (prt[pl.ds(pl.multiple_of(x * 32, 32), 32), :] - total).astype(BF)
    pf = mm_nt(res, plinv[0]).astype(BF)

    def unit(pos):
        t = pos // 2
        return (core * 4 + t) * 32 + bx[t][0] * 8 + ax[t][0] * 2 + pos % 2

    sol[...] = mm_nt(pf, puinv[0]).astype(BF)
    gath[unit(0)] = sol[...]

    for d in (4, 3, 5, 2, 6, 1, 7):
        pos = NEAR.index(8 - d)
        send(sol, gath.at[unit(pos)], d_z[d], "bz", pos // 2)

    def share(ref_slice, dev_, *key):
        send(gath.at[ref_slice], gath.at[ref_slice], dev_, *key)

    def piece(t, e, d):
        return pl.ds((core * 4 + t) * 32 + bx[t][e] * 8 + ax[t][d] * 2, 2)

    def whole_row(t, e, n=8):
        return pl.ds((core * 4 + t) * 32 + bx[t][e] * 8, n)

    def along_a(t, e):
        for d in order[:3]:
            share(piece(t, e, 0), d_a[t][d], "ba", t, e)

    def along_b(t):
        new = pl.ds(unit(0) + 1, 1) if t == 0 else piece(t, 0, 0)
        arrived(gath.at[new], "bz", t)
        for e in order[:3]:
            share(piece(t, 0, 0), d_b[t][e], "bb", t, e)
        along_a(t, 0)

    def along_row(t, e):
        arrived(gath.at[piece(t, e, 0)], "bb", t, 4 - e)
        along_a(t, e)

    def across(t, e):
        arrived(gath.at[whole_row(t, e, 6)], "ba", t, e)
        share(whole_row(t, e), d_sib, "o")

    for t in PARTS:
        along_b(t)
    for t in (0, 1):
        for e in (1, 3, 2):
            along_row(t, e)
    for t in (0, 1):
        across(t, 0)
    for t in (2, 3):
        for e in (1, 3, 2):
            along_row(t, e)
    for t in (0, 1):
        for e in (1, 3, 2):
            across(t, e)
    for e in (0, 1, 3, 2):
        for t in (2, 3):
            across(t, e)
    arrived(gath.at[pl.ds(flip * 128, 128)], "o")
    most = snd.at[pl.ds(0, 3)]
    for i, sent in enumerate((sib, most, snd2, zr_out, zr_out, snd2, most, sib)):
        remote(sent, sent, i, 0, d_sib).wait_send()


def backward_kernel(po, gath, ufwd, mat, out_h, psol_h, out, psol, sem):
    col = lax.axis_index("col")
    z = lax.rem(lax.div(col, 2), 8)
    psol[0] = parent_of_units(gath, col, z).T
    copies = []

    def put(src, dst):
        cp = pltpu.make_async_copy(src, dst, sem.at[len(copies)])
        cp.start()
        copies.append(cp)

    put(psol, psol_h)
    for k in range(CHUNKS):
        for c in range(k * GRP, (k + 1) * GRP):
            s = parent_of_units(gath, po[c], z)
            out[c] = (ufwd[c] - mm_nt(mat[c], s)).astype(BF)
        part = pl.ds(k * GRP, GRP)
        put(out.at[part], out_h.at[part])
    for cp in copies:
        cp.wait()


def on_device(
    child_rhs,
    parent_rhs,
    child_lower_inv,
    child_lower_off,
    child_upper_inv,
    child_upper_off,
    parent_lower_inv,
    parent_upper_inv,
    parent_of,
):
    mats = lambda: pltpu.VMEM((NCH, 128, 128), BF)
    one = lambda: pltpu.VMEM((1, 128, 128), BF)
    units = lambda *k: pltpu.VMEM((*k, 32, 128), BF)
    smem = pl.BlockSpec(memory_space=pltpu.SMEM)
    vmem = pl.BlockSpec(memory_space=pltpu.VMEM)
    hbm = pl.BlockSpec(memory_space=pl.ANY)
    gath, ufwd, mat = pl.pallas_call(
        forward_kernel,
        out_shape=(
            jax.ShapeDtypeStruct((256, 32, 128), BF),
            jax.ShapeDtypeStruct((NCH, 128, 128), F32),
            jax.ShapeDtypeStruct((NCH, 128, 128), BF),
        ),
        in_specs=[hbm] * 9,
        out_specs=(vmem, vmem, vmem),
        scratch_shapes=[
            mats(),
            mats(),
            mats(),
            mats(),
            mats(),
            one(),
            one(),
            one(),
            mats(),
            pltpu.VMEM((NCH + 1, 128, 128), F32),
            pltpu.VMEM((1, NCH), jnp.int32),
            pltpu.VMEM((1, 128), jnp.int32),
            pltpu.SMEM((1, 128), jnp.int32),
            units(4, 32),
            units(4, 32),
            units(4, 32),
            units(4, 4, 3, 2),
            units(4, 3, 2),
            units(4, 3, 2),
            pltpu.VMEM((8, 32, 128), F32),
            units(7),
            units(7),
            units(),
            pltpu.VMEM((128, 128), F32),
            pltpu.SemaphoreType.DMA((3 * CHUNKS + 9,)),
            pltpu.SemaphoreType.DMA((1,)),
            pltpu.SemaphoreType.DMA((8,)),
            pltpu.SemaphoreType.DMA((70,)),
        ],
        compiler_params=pltpu.CompilerParams(
            collective_id=0, has_side_effects=True, vmem_limit_bytes=40 * 2**20
        ),
    )(
        *[
            pltpu.with_memory_space_constraint(v, pltpu.HBM)
            for v in (
                parent_of.reshape(1, NCH),
                child_rhs,
                parent_rhs,
                child_lower_inv,
                child_lower_off,
                child_upper_inv,
                child_upper_off,
                parent_lower_inv,
                parent_upper_inv,
            )
        ]
    )
    return pl.pallas_call(
        backward_kernel,
        out_shape=(
            jax.ShapeDtypeStruct(child_rhs.shape, BF),
            jax.ShapeDtypeStruct(parent_rhs.shape, BF),
        ),
        in_specs=[smem, vmem, vmem, vmem],
        out_specs=(hbm, hbm),
        scratch_shapes=[mats(), one(), pltpu.SemaphoreType.DMA((CHUNKS + 1,))],
        compiler_params=pltpu.CompilerParams(vmem_limit_bytes=16 * 2**20),
    )(parent_of, gath, ufwd, mat)


def solution(mesh):
    child = P(("row", "col"), None, None)
    par = P("col", None, None)
    return jax.shard_map(
        on_device,
        mesh=mesh,
        in_specs=(child, par, child, child, child, child, par, par, P(("row", "col"))),
        out_specs=(child, par),
        check_vma=False,
    )
```

```python
import jax
import jax.numpy as jnp
from jax import lax
from jax.experimental import pallas as pl
from jax.experimental.pallas import tpu as pltpu
from jax.sharding import PartitionSpec as P

BF = jnp.bfloat16
F32 = jnp.float32
MESH = pl.DeviceIdType.MESH
NCH = 48
GRP = 8
CHUNKS = NCH // GRP
NT = (((1,), (1,)), ((), ()))


def mm(a, b):
    return jnp.dot(a, b, preferred_element_type=F32)


def mm_nt(a, b):
    return lax.dot_general(a, b, NT, preferred_element_type=F32)


def loop(n, body, unroll=1):
    def step(i, carry):
        body(i)
        return carry

    lax.fori_loop(0, n, step, 0, unroll=unroll)


NEAR = (0, 1, 7, 2, 6, 3, 5, 4)
PARTS = range(4)


def place_of(p, z):
    h, pz, y = lax.rem(p, 2), lax.rem(lax.div(p, 2), 8), lax.div(p, 16)
    far = lax.rem(pz - z + 8, 8)
    pos = jnp.maximum(jnp.minimum(2 * far - 1, 16 - 2 * far), 0)
    t, odd = lax.div(pos, 2), lax.rem(lax.div(pos, 2), 2)
    first = (h * 4 + t) * 32 + lax.rem(pos, 2) + (1 - odd) * y * 8 + odd * y * 2
    return first, (1 - odd) * 2 + odd * 8


def parent_of_units(gath, p, z):
    first, step = place_of(p, z)
    return jnp.concatenate([gath[first + q * step] for q in range(4)], axis=0)


def forward_kernel(
    po_h,
    rhs_h,
    prhs_h,
    linv_h,
    loff_h,
    uinv_h,
    uoff_h,
    plinv_h,
    puinv_h,
    gath,
    ufwd,
    mat,
    rhs,
    linv,
    loff,
    uinv,
    uoff,
    prhs,
    plinv,
    puinv,
    fwd,
    run,
    pov,
    tabv,
    tab,
    sib,
    sibr,
    snd,
    fin,
    snd2,
    gin,
    held,
    zr_out,
    zr,
    sol,
    prt,
    load_sem,
    tab_sem,
    send_sem,
    recv_sem,
):
    x = lax.axis_index("row")
    col = lax.axis_index("col")
    core = lax.rem(col, 2)
    z = lax.rem(lax.div(col, 2), 8)
    y = lax.div(col, 16)
    flip = 1 - core

    def dev(x_, y_, z_, c_):
        return (x_, y_ * 16 + z_ * 2 + c_)

    def mod4(v):
        return lax.rem(v, 4)

    d_sib = dev(x, y, z, flip)
    d_x = [dev(mod4(x + d), y, z, core) for d in range(4)]
    d_y = [dev(x, mod4(y + d), z, core) for d in range(4)]
    zs = [lax.rem(z + d, 8) for d in range(8)]
    d_z = [dev(x, y, zs[d], core) for d in range(8)]
    d_a, d_b = (d_x, d_y) * 2, (d_y, d_x) * 2
    x_at, y_at = [mod4(x + d) for d in range(4)], [mod4(y + d) for d in range(4)]
    ax, bx = (x_at, y_at) * 2, (y_at, x_at) * 2

    group = [0]

    def load(*pairs, whole=None):
        sem = load_sem.at[group[0]]
        group[0] += 1
        for src, dst in pairs:
            pltpu.make_async_copy(src, dst, sem).start()
        return pltpu.make_async_copy(*(whole or pairs[0]), sem)

    starts = [0, 4] + list(range(8, NCH + 1, GRP))
    spans = list(zip(starts[:-1], starts[1:], strict=True))

    def load_span(lo, hi):
        part, size = pl.ds(lo, hi - lo), pl.ds(0, 3 * (hi - lo))
        pairs = ((linv_h, linv), (rhs_h, rhs), (loff_h, loff))
        return load(
            *[(src.at[part], dst.at[part]) for src, dst in pairs],
            whole=(linv_h.at[size], linv.at[size]),
        )

    po_load = load((po_h, pov))
    span_loads = [load_span(*span) for span in spans]
    upper_loads = [load((uinv_h, uinv)), load((uoff_h, uoff))]
    parent_load = load(
        (prhs_h, prhs),
        (plinv_h, plinv),
        (puinv_h, puinv),
        whole=(linv_h.at[pl.ds(0, 3)], linv.at[pl.ds(0, 3)]),
    )

    barrier = pltpu.get_barrier_semaphore()
    peers = [d_sib] + d_x[1:] + d_y[1:] + d_z[1:]
    for peer in peers:
        pl.semaphore_signal(barrier, inc=1, device_id=peer, device_id_type=MESH)

    run[NCH] = jnp.zeros((128, 128), F32)

    def table():
        po_load.wait()
        mine = jnp.concatenate(
            [pov[...], jnp.full((1, 128 - NCH), -1, jnp.int32)], axis=1
        )
        rows = jnp.broadcast_to(mine, (128, 128))
        lane = lax.broadcasted_iota(jnp.int32, (128, 128), 1)
        child = lax.broadcasted_iota(jnp.int32, (128, 128), 0)
        label = jnp.where(lane < 64, rows, lane - 64)
        hit = (rows.T == label) & (child < jnp.where(lane < 64, lane, NCH))
        last = jnp.max(jnp.where(hit, child, -1), axis=0, keepdims=True)
        tabv[...] = jnp.where(last < 0, NCH, last)
        cp = pltpu.make_async_copy(tabv, tab, tab_sem.at[0])
        cp.start()
        return cp

    tab_copy = table()
    for k, (lo, hi) in enumerate(spans):
        span_loads[k].wait()
        terms = []
        for c in range(lo, hi):
            f = mm(linv[c], rhs[c]).astype(BF)
            fwd[c] = f
            term = mm_nt(f.T, loff[c])
            if k < 2:
                run[c] = term
            terms.append(term)
        if k == 1:
            tab_copy.wait()
            for c in range(hi):
                run[c] = run[c] + run[tab[0, c]]
        elif k > 1:
            for c in range(lo, hi):
                run[c] = terms[c - lo] + run[tab[0, c]]

    def mine_of(t, b_, a_, zz, core_):
        x_, y_ = (b_, a_) if t % 2 else (a_, b_)
        row = pl.multiple_of(x_ * 32, 32)
        last_ = tab[0, 64 + y_ * 16 + zs[NEAR[t * 2 + zz]] * 2 + core_]
        return run[last_, pl.ds(row, 32), :]

    stages = ("s0", "f", "g", "z", "bz", "bb", "ba", "o")
    slots = {}

    def slot(*key):
        return slots.setdefault(key, len(slots))

    def remote(src, dst, sent, got, dev_):
        return pltpu.make_async_remote_copy(
            src_ref=src,
            dst_ref=dst,
            send_sem=send_sem.at[sent],
            recv_sem=recv_sem.at[got],
            device_id=dev_,
            device_id_type=MESH,
        )

    def send(src, dst, dev_, stage, *key):
        remote(src, dst, stages.index(stage), slot(stage, *key), dev_).start()

    def arrived(dst, *key):
        remote(dst, dst, 0, slot(*key), d_sib).wait_recv()

    order = (2, 1, 3, 0)
    far_first = (3, 2, 1, 0)
    rows_first = [(t, e) for ts in ((3, 2), (1, 0)) for e in order[:3] for t in ts]
    rows_first += [(t, 0) for t in far_first]

    def row_of(b_):
        return pl.ds(b_ * 8, 8)

    waited = False
    for t, e in rows_first:
        b_ = bx[t][e]
        for a_ in range(4):
            for zz in range(2):
                v = mine_of(t, b_, a_, zz, flip)
                sib[t, b_ * 8 + a_ * 2 + zz] = v.astype(BF)
        if not waited:
            pl.semaphore_wait(barrier, len(peers))
            waited = True
        rows_ = row_of(b_)
        send(sib.at[t, rows_], sibr.at[t, rows_], d_sib, "s0", t, e)

    for t, e in rows_first:
        b_ = bx[t][e]
        arrived(sibr.at[t, row_of(b_)], "s0", t, e)
        for d in order[:3]:
            a_ = ax[t][d]
            for zz in range(2):
                u = b_ * 8 + a_ * 2 + zz
                v = mine_of(t, b_, a_, zz, core) + sibr[t, u].astype(F32)
                snd[t, u] = v.astype(BF)
            src = snd.at[t, pl.ds(b_ * 8 + a_ * 2, 2)]
            send(src, fin.at[t, e, d - 1], d_a[t][d], "f", t, e)

    def at_a(t, e, zz):
        b_, a_ = bx[t][e], ax[t][0]
        v = mine_of(t, b_, a_, zz, core) + sibr[t, b_ * 8 + a_ * 2 + zz].astype(F32)
        for d in range(3):
            v = v + fin[t, e, d, zz].astype(F32)
        return v

    for t, e in rows_first:
        arrived(fin.at[t, e], "f", t, e)
        for zz in range(2):
            v = at_a(t, e, zz)
            if e == 0:
                held[t * 2 + zz] = v
            else:
                snd2[t, e - 1, zz] = v.astype(BF)
        if e:
            send(snd2.at[t, e - 1], gin.at[t, e - 1], d_b[t][e], "g", t)

    for t in far_first:
        arrived(gin.at[t], "g", t)
        for zz in (1, 0):
            pos = t * 2 + zz
            v = held[pos]
            for e in range(3):
                v = v + gin[t, e, zz].astype(F32)
            if pos == 0:
                total = v
                continue
            d = NEAR[pos]
            zr_out[d - 1] = v.astype(BF)
            send(zr_out.at[d - 1], zr.at[d - 1], d_z[d], "z")
    held[0] = total

    parent_load.wait()
    prt[...] = prhs[0].astype(F32).T
    for cp in upper_loads:
        cp.wait()

    def prepare(i):
        for j in range(4):
            c = i * 4 + j
            ui = uinv[c]
            ufwd[c] = mm(ui, fwd[c])
            mat[c] = mm(ui, uoff[c]).astype(BF)

    loop(NCH // 4, prepare)

    total = held[0]
    arrived(zr, "z")
    for d in range(1, 8):
        total = total + zr[d - 1].astype(F32)

    res = (prt[pl.ds(pl.multiple_of(x * 32, 32), 32), :] - total).astype(BF)
    pf = mm_nt(res, plinv[0]).astype(BF)

    def unit(pos):
        t = pos // 2
        return (core * 4 + t) * 32 + bx[t][0] * 8 + ax[t][0] * 2 + pos % 2

    sol[...] = mm_nt(pf, puinv[0]).astype(BF)
    gath[unit(0)] = sol[...]

    for d in (4, 3, 5, 2, 6, 1, 7):
        pos = NEAR.index(8 - d)
        send(sol, gath.at[unit(pos)], d_z[d], "bz", pos // 2)

    def share(ref_slice, dev_, *key):
        send(gath.at[ref_slice], gath.at[ref_slice], dev_, *key)

    def piece(t, e, d):
        return pl.ds((core * 4 + t) * 32 + bx[t][e] * 8 + ax[t][d] * 2, 2)

    def whole_row(t, e, n=8):
        return pl.ds((core * 4 + t) * 32 + bx[t][e] * 8, n)

    def along_a(t, e):
        for d in order[:3]:
            share(piece(t, e, 0), d_a[t][d], "ba", t, e)

    def along_b(t):
        new = pl.ds(unit(0) + 1, 1) if t == 0 else piece(t, 0, 0)
        arrived(gath.at[new], "bz", t)
        for e in order[:3]:
            share(piece(t, 0, 0), d_b[t][e], "bb", t, e == 2)
        along_a(t, 0)

    def along_rows(t):
        arrived(gath.at[whole_row(t, 0, 4)], "bb", t, False)
        along_a(t, 1)
        along_a(t, 3)
        arrived(gath.at[piece(t, 2, 0)], "bb", t, True)
        along_a(t, 2)

    def across(t, e):
        arrived(gath.at[whole_row(t, e, 6)], "ba", t, e)
        share(whole_row(t, e), d_sib, "o")

    for t in PARTS:
        along_b(t)
    for t in (0, 1):
        along_rows(t)
    for t in (0, 1):
        across(t, 0)
    for t in (2, 3):
        along_rows(t)
    for t in (0, 1):
        for e in (1, 3, 2):
            across(t, e)
    for e in (0, 1, 3, 2):
        for t in (2, 3):
            across(t, e)
    arrived(gath.at[pl.ds(flip * 128, 128)], "o")
    most = snd.at[pl.ds(0, 3)]
    for i, sent in enumerate((sib, most, snd2, zr_out, zr_out, snd2, most, sib)):
        remote(sent, sent, i, 0, d_sib).wait_send()


def backward_kernel(po, gath, ufwd, mat, out_h, psol_h, out, psol, sem):
    col = lax.axis_index("col")
    z = lax.rem(lax.div(col, 2), 8)
    psol[0] = parent_of_units(gath, col, z).T
    pltpu.make_async_copy(psol, psol_h, sem.at[0]).start()
    for k in range(CHUNKS):
        for c in range(k * GRP, (k + 1) * GRP):
            s = parent_of_units(gath, po[c], z)
            out[c] = (ufwd[c] - mm_nt(mat[c], s)).astype(BF)
        part = pl.ds(k * GRP, GRP)
        pltpu.make_async_copy(out.at[part], out_h.at[part], sem.at[1]).start()
    pltpu.make_async_copy(psol, psol_h, sem.at[0]).wait()
    pltpu.make_async_copy(out, out_h, sem.at[1]).wait()


def on_device(
    child_rhs,
    parent_rhs,
    child_lower_inv,
    child_lower_off,
    child_upper_inv,
    child_upper_off,
    parent_lower_inv,
    parent_upper_inv,
    parent_of,
):
    mats = lambda: pltpu.VMEM((NCH, 128, 128), BF)
    one = lambda: pltpu.VMEM((1, 128, 128), BF)
    units = lambda *k: pltpu.VMEM((*k, 32, 128), BF)
    smem = pl.BlockSpec(memory_space=pltpu.SMEM)
    vmem = pl.BlockSpec(memory_space=pltpu.VMEM)
    hbm = pl.BlockSpec(memory_space=pl.ANY)
    gath, ufwd, mat = pl.pallas_call(
        forward_kernel,
        out_shape=(
            jax.ShapeDtypeStruct((256, 32, 128), BF),
            jax.ShapeDtypeStruct((NCH, 128, 128), F32),
            jax.ShapeDtypeStruct((NCH, 128, 128), BF),
        ),
        in_specs=[hbm] * 9,
        out_specs=(vmem, vmem, vmem),
        scratch_shapes=[
            mats(),
            mats(),
            mats(),
            mats(),
            mats(),
            one(),
            one(),
            one(),
            mats(),
            pltpu.VMEM((NCH + 1, 128, 128), F32),
            pltpu.VMEM((1, NCH), jnp.int32),
            pltpu.VMEM((1, 128), jnp.int32),
            pltpu.SMEM((1, 128), jnp.int32),
            units(4, 32),
            units(4, 32),
            units(4, 32),
            units(4, 4, 3, 2),
            units(4, 3, 2),
            units(4, 3, 2),
            pltpu.VMEM((8, 32, 128), F32),
            units(7),
            units(7),
            units(),
            pltpu.VMEM((128, 128), F32),
            pltpu.SemaphoreType.DMA((CHUNKS + 5,)),
            pltpu.SemaphoreType.DMA((1,)),
            pltpu.SemaphoreType.DMA((8,)),
            pltpu.SemaphoreType.DMA((66,)),
        ],
        compiler_params=pltpu.CompilerParams(
            collective_id=0, has_side_effects=True, vmem_limit_bytes=40 * 2**20
        ),
    )(
        *[
            pltpu.with_memory_space_constraint(v, pltpu.HBM)
            for v in (
                parent_of.reshape(1, NCH),
                child_rhs,
                parent_rhs,
                child_lower_inv,
                child_lower_off,
                child_upper_inv,
                child_upper_off,
                parent_lower_inv,
                parent_upper_inv,
            )
        ]
    )
    return pl.pallas_call(
        backward_kernel,
        out_shape=(
            jax.ShapeDtypeStruct(child_rhs.shape, BF),
            jax.ShapeDtypeStruct(parent_rhs.shape, BF),
        ),
        in_specs=[smem, vmem, vmem, vmem],
        out_specs=(hbm, hbm),
        scratch_shapes=[mats(), one(), pltpu.SemaphoreType.DMA((2,))],
        compiler_params=pltpu.CompilerParams(vmem_limit_bytes=16 * 2**20),
    )(parent_of, gath, ufwd, mat)


def solution(mesh):
    child = P(("row", "col"), None, None)
    par = P("col", None, None)
    return jax.shard_map(
        on_device,
        mesh=mesh,
        in_specs=(child, par, child, child, child, child, par, par, P(("row", "col"))),
        out_specs=(child, par),
        check_vma=False,
    )
```

```python
import jax
import jax.numpy as jnp
from jax import lax
from jax.experimental import pallas as pl
from jax.experimental.pallas import tpu as pltpu
from jax.sharding import PartitionSpec as P

BF = jnp.bfloat16
F32 = jnp.float32
MESH = pl.DeviceIdType.MESH
NCH = 48
GRP = 8
CHUNKS = NCH // GRP
NT = (((1,), (1,)), ((), ()))


def mm(a, b):
    return jnp.dot(a, b, preferred_element_type=F32)


def mm_nt(a, b):
    return lax.dot_general(a, b, NT, preferred_element_type=F32)


def loop(n, body, unroll=1):
    def step(i, carry):
        body(i)
        return carry

    lax.fori_loop(0, n, step, 0, unroll=unroll)


NEAR = (0, 1, 7, 2, 6, 3, 5, 4)
PARTS = range(4)


def place_of(p, z):
    h, pz, y = lax.rem(p, 2), lax.rem(lax.div(p, 2), 8), lax.div(p, 16)
    far = lax.rem(pz - z + 8, 8)
    pos = jnp.maximum(jnp.minimum(2 * far - 1, 16 - 2 * far), 0)
    t, odd = lax.div(pos, 2), lax.rem(lax.div(pos, 2), 2)
    first = (h * 4 + t) * 32 + lax.rem(pos, 2) + (1 - odd) * y * 8 + odd * y * 2
    return first, (1 - odd) * 2 + odd * 8


def parent_of_units(gath, p, z):
    first, step = place_of(p, z)
    return jnp.concatenate([gath[first + q * step] for q in range(4)], axis=0)


def forward_kernel(
    po_h,
    rhs_h,
    prhs_h,
    linv_h,
    loff_h,
    uinv_h,
    uoff_h,
    plinv_h,
    puinv_h,
    gath,
    ufwd,
    mat,
    rhs,
    linv,
    loff,
    uinv,
    uoff,
    prhs,
    plinv,
    puinv,
    fwd,
    run,
    pov,
    tabv,
    tab,
    sib,
    sibr,
    snd,
    fin,
    snd2,
    gin,
    held,
    zr_out,
    zr,
    sol,
    prt,
    load_sem,
    tab_sem,
    send_sem,
    recv_sem,
):
    x = lax.axis_index("row")
    col = lax.axis_index("col")
    core = lax.rem(col, 2)
    z = lax.rem(lax.div(col, 2), 8)
    y = lax.div(col, 16)
    flip = 1 - core

    def dev(x_, y_, z_, c_):
        return (x_, y_ * 16 + z_ * 2 + c_)

    def mod4(v):
        return lax.rem(v, 4)

    d_sib = dev(x, y, z, flip)
    d_x = [dev(mod4(x + d), y, z, core) for d in range(4)]
    d_y = [dev(x, mod4(y + d), z, core) for d in range(4)]
    zs = [lax.rem(z + d, 8) for d in range(8)]
    d_z = [dev(x, y, zs[d], core) for d in range(8)]
    d_a, d_b = (d_x, d_y) * 2, (d_y, d_x) * 2
    o_x = [dev(mod4(x + d), y, z, flip) for d in range(4)]
    o_y = [dev(x, mod4(y + d), z, flip) for d in range(4)]
    o_a = (o_x, o_y) * 2
    x_at, y_at = [mod4(x + d) for d in range(4)], [mod4(y + d) for d in range(4)]
    ax, bx = (x_at, y_at) * 2, (y_at, x_at) * 2

    group = [0]

    def load(*pairs, whole=None):
        sem = load_sem.at[group[0]]
        group[0] += 1
        for src, dst in pairs:
            pltpu.make_async_copy(src, dst, sem).start()
        return pltpu.make_async_copy(*(whole or pairs[0]), sem)

    starts = [0, 4] + list(range(8, NCH + 1, GRP))
    spans = list(zip(starts[:-1], starts[1:], strict=True))

    def load_span(lo, hi):
        part, size = pl.ds(lo, hi - lo), pl.ds(0, 3 * (hi - lo))
        pairs = ((linv_h, linv), (rhs_h, rhs), (loff_h, loff))
        return load(
            *[(src.at[part], dst.at[part]) for src, dst in pairs],
            whole=(linv_h.at[size], linv.at[size]),
        )

    po_load = load((po_h, pov))
    span_loads = [load_span(*span) for span in spans]
    upper_loads = [load((uinv_h, uinv)), load((uoff_h, uoff))]
    parent_load = load(
        (prhs_h, prhs),
        (plinv_h, plinv),
        (puinv_h, puinv),
        whole=(linv_h.at[pl.ds(0, 3)], linv.at[pl.ds(0, 3)]),
    )

    barrier = pltpu.get_barrier_semaphore()
    peers = o_x + o_y[1:] + d_x[1:] + d_y[1:] + d_z[1:]
    for peer in peers:
        pl.semaphore_signal(barrier, inc=1, device_id=peer, device_id_type=MESH)

    run[NCH] = jnp.zeros((128, 128), F32)

    def table():
        po_load.wait()
        mine = jnp.concatenate(
            [pov[...], jnp.full((1, 128 - NCH), -1, jnp.int32)], axis=1
        )
        rows = jnp.broadcast_to(mine, (128, 128))
        lane = lax.broadcasted_iota(jnp.int32, (128, 128), 1)
        child = lax.broadcasted_iota(jnp.int32, (128, 128), 0)
        label = jnp.where(lane < 64, rows, lane - 64)
        hit = (rows.T == label) & (child < jnp.where(lane < 64, lane, NCH))
        last = jnp.max(jnp.where(hit, child, -1), axis=0, keepdims=True)
        tabv[...] = jnp.where(last < 0, NCH, last)
        cp = pltpu.make_async_copy(tabv, tab, tab_sem.at[0])
        cp.start()
        return cp

    tab_copy = table()
    for k, (lo, hi) in enumerate(spans):
        span_loads[k].wait()
        terms = []
        for c in range(lo, hi):
            f = mm(linv[c], rhs[c]).astype(BF)
            fwd[c] = f
            term = mm_nt(f.T, loff[c])
            if k < 2:
                run[c] = term
            terms.append(term)
        if k == 1:
            tab_copy.wait()
            for c in range(hi):
                run[c] = run[c] + run[tab[0, c]]
        elif k > 1:
            for c in range(lo, hi):
                run[c] = terms[c - lo] + run[tab[0, c]]

    def mine_of(t, b_, a_, zz, core_):
        x_, y_ = (b_, a_) if t % 2 else (a_, b_)
        row = pl.multiple_of(x_ * 32, 32)
        last_ = tab[0, 64 + y_ * 16 + zs[NEAR[t * 2 + zz]] * 2 + core_]
        return run[last_, pl.ds(row, 32), :]

    stages = ("s0", "f", "g", "z", "bz", "bb", "ba", "o")
    slots = {}

    def slot(*key):
        return slots.setdefault(key, len(slots))

    def remote(src, dst, sent, got, dev_):
        return pltpu.make_async_remote_copy(
            src_ref=src,
            dst_ref=dst,
            send_sem=send_sem.at[sent],
            recv_sem=recv_sem.at[got],
            device_id=dev_,
            device_id_type=MESH,
        )

    def send(src, dst, dev_, stage, *key):
        remote(src, dst, stages.index(stage), slot(stage, *key), dev_).start()

    def arrived(dst, *key):
        remote(dst, dst, 0, slot(*key), d_sib).wait_recv()

    order = (2, 1, 3, 0)
    far_first = (3, 2, 1, 0)
    rows_first = [(t, e) for ts in ((3, 2), (1, 0)) for e in order[:3] for t in ts]
    rows_first += [(t, 0) for t in far_first]

    def row_of(b_):
        return pl.ds(b_ * 8, 8)

    waited = False
    for t, e in rows_first:
        b_ = bx[t][e]
        for a_ in range(4):
            for zz in range(2):
                v = mine_of(t, b_, a_, zz, flip)
                sib[t, b_ * 8 + a_ * 2 + zz] = v.astype(BF)
        if not waited:
            pl.semaphore_wait(barrier, len(peers))
            waited = True
        rows_ = row_of(b_)
        send(sib.at[t, rows_], sibr.at[t, rows_], d_sib, "s0", t, e)

    for t, e in rows_first:
        b_ = bx[t][e]
        arrived(sibr.at[t, row_of(b_)], "s0", t, e)
        for d in order[:3]:
            a_ = ax[t][d]
            for zz in range(2):
                u = b_ * 8 + a_ * 2 + zz
                v = mine_of(t, b_, a_, zz, core) + sibr[t, u].astype(F32)
                snd[t, u] = v.astype(BF)
            src = snd.at[t, pl.ds(b_ * 8 + a_ * 2, 2)]
            send(src, fin.at[t, e, d - 1], d_a[t][d], "f", t, e)

    def at_a(t, e, zz):
        b_, a_ = bx[t][e], ax[t][0]
        v = mine_of(t, b_, a_, zz, core) + sibr[t, b_ * 8 + a_ * 2 + zz].astype(F32)
        for d in range(3):
            v = v + fin[t, e, d, zz].astype(F32)
        return v

    for t, e in rows_first:
        arrived(fin.at[t, e], "f", t, e)
        for zz in range(2):
            v = at_a(t, e, zz)
            if e == 0:
                held[t * 2 + zz] = v
            else:
                snd2[t, e - 1, zz] = v.astype(BF)
        if e:
            send(snd2.at[t, e - 1], gin.at[t, e - 1], d_b[t][e], "g", t)

    for t in far_first:
        arrived(gin.at[t], "g", t)
        for zz in (1, 0):
            pos = t * 2 + zz
            v = held[pos]
            for e in range(3):
                v = v + gin[t, e, zz].astype(F32)
            if pos == 0:
                total = v
                continue
            d = NEAR[pos]
            zr_out[d - 1] = v.astype(BF)
            send(zr_out.at[d - 1], zr.at[d - 1], d_z[d], "z")
    held[0] = total

    parent_load.wait()
    prt[...] = prhs[0].astype(F32).T
    for cp in upper_loads:
        cp.wait()

    def prepare(i):
        for j in range(4):
            c = i * 4 + j
            ui = uinv[c]
            ufwd[c] = mm(ui, fwd[c])
            mat[c] = mm(ui, uoff[c]).astype(BF)

    loop(NCH // 4, prepare)

    total = held[0]
    arrived(zr, "z")
    for d in range(1, 8):
        total = total + zr[d - 1].astype(F32)

    res = (prt[pl.ds(pl.multiple_of(x * 32, 32), 32), :] - total).astype(BF)
    pf = mm_nt(res, plinv[0]).astype(BF)

    def unit(pos):
        t = pos // 2
        return (core * 4 + t) * 32 + bx[t][0] * 8 + ax[t][0] * 2 + pos % 2

    sol[...] = mm_nt(pf, puinv[0]).astype(BF)
    gath[unit(0)] = sol[...]

    for d in (4, 3, 5, 2, 6, 1, 7):
        pos = NEAR.index(8 - d)
        send(sol, gath.at[unit(pos)], d_z[d], "bz", pos // 2)

    def share(ref_slice, dev_, *key):
        send(gath.at[ref_slice], gath.at[ref_slice], dev_, *key)

    def piece(t, e, d):
        return pl.ds((core * 4 + t) * 32 + bx[t][e] * 8 + ax[t][d] * 2, 2)

    def whole_row(t, e, n=8):
        return pl.ds((core * 4 + t) * 32 + bx[t][e] * 8, n)

    def along_a(t, e):
        for d in order[:3]:
            share(piece(t, e, 0), d_a[t][d], "ba", t, e)

    def along_b(t):
        new = pl.ds(unit(0) + 1, 1) if t == 0 else piece(t, 0, 0)
        arrived(gath.at[new], "bz", t)
        for e in order[:3]:
            share(piece(t, 0, 0), d_b[t][e], "bb", t, e == 2)
        along_a(t, 0)

    def along_rows(t):
        arrived(gath.at[whole_row(t, 0, 4)], "bb", t, False)
        along_a(t, 1)
        along_a(t, 3)
        arrived(gath.at[piece(t, 2, 0)], "bb", t, True)
        along_a(t, 2)
        if t > 1:
            for d in (2, 1, 3, 0):
                share(piece(t, 2, 0), o_a[t][d], "o")

    def across(t, e):
        arrived(gath.at[whole_row(t, e, 6)], "ba", t, e)
        if (t > 1) and (e == 2):
            return
        share(whole_row(t, e), d_sib, "o")

    for t in PARTS:
        along_b(t)
    for t in (0, 1):
        along_rows(t)
    for t in (0, 1):
        across(t, 0)
    for t in (2, 3):
        along_rows(t)
    for t in (0, 1):
        for e in (1, 3, 2):
            across(t, e)
    for e in (0, 1, 3, 2):
        for t in (2, 3):
            across(t, e)
    arrived(gath.at[pl.ds(flip * 128, 128)], "o")
    most = snd.at[pl.ds(0, 3)]
    for i, sent in enumerate((sib, most, snd2, zr_out, zr_out, snd2, most, sib)):
        remote(sent, sent, i, 0, d_sib).wait_send()


def backward_kernel(po, gath, ufwd, mat, out_h, psol_h, out, psol, sem):
    col = lax.axis_index("col")
    z = lax.rem(lax.div(col, 2), 8)
    psol[0] = parent_of_units(gath, col, z).T
    pltpu.make_async_copy(psol, psol_h, sem.at[0]).start()
    for k in range(CHUNKS):
        for c in range(k * GRP, (k + 1) * GRP):
            s = parent_of_units(gath, po[c], z)
            out[c] = (ufwd[c] - mm_nt(mat[c], s)).astype(BF)
        part = pl.ds(k * GRP, GRP)
        pltpu.make_async_copy(out.at[part], out_h.at[part], sem.at[1]).start()
    pltpu.make_async_copy(psol, psol_h, sem.at[0]).wait()
    pltpu.make_async_copy(out, out_h, sem.at[1]).wait()


def on_device(
    child_rhs,
    parent_rhs,
    child_lower_inv,
    child_lower_off,
    child_upper_inv,
    child_upper_off,
    parent_lower_inv,
    parent_upper_inv,
    parent_of,
):
    mats = lambda: pltpu.VMEM((NCH, 128, 128), BF)
    one = lambda: pltpu.VMEM((1, 128, 128), BF)
    units = lambda *k: pltpu.VMEM((*k, 32, 128), BF)
    smem = pl.BlockSpec(memory_space=pltpu.SMEM)
    vmem = pl.BlockSpec(memory_space=pltpu.VMEM)
    hbm = pl.BlockSpec(memory_space=pl.ANY)
    gath, ufwd, mat = pl.pallas_call(
        forward_kernel,
        out_shape=(
            jax.ShapeDtypeStruct((256, 32, 128), BF),
            jax.ShapeDtypeStruct((NCH, 128, 128), F32),
            jax.ShapeDtypeStruct((NCH, 128, 128), BF),
        ),
        in_specs=[hbm] * 9,
        out_specs=(vmem, vmem, vmem),
        scratch_shapes=[
            mats(),
            mats(),
            mats(),
            mats(),
            mats(),
            one(),
            one(),
            one(),
            mats(),
            pltpu.VMEM((NCH + 1, 128, 128), F32),
            pltpu.VMEM((1, NCH), jnp.int32),
            pltpu.VMEM((1, 128), jnp.int32),
            pltpu.SMEM((1, 128), jnp.int32),
            units(4, 32),
            units(4, 32),
            units(4, 32),
            units(4, 4, 3, 2),
            units(4, 3, 2),
            units(4, 3, 2),
            pltpu.VMEM((8, 32, 128), F32),
            units(7),
            units(7),
            units(),
            pltpu.VMEM((128, 128), F32),
            pltpu.SemaphoreType.DMA((CHUNKS + 5,)),
            pltpu.SemaphoreType.DMA((1,)),
            pltpu.SemaphoreType.DMA((8,)),
            pltpu.SemaphoreType.DMA((66,)),
        ],
        compiler_params=pltpu.CompilerParams(
            collective_id=0, has_side_effects=True, vmem_limit_bytes=40 * 2**20
        ),
    )(
        *[
            pltpu.with_memory_space_constraint(v, pltpu.HBM)
            for v in (
                parent_of.reshape(1, NCH),
                child_rhs,
                parent_rhs,
                child_lower_inv,
                child_lower_off,
                child_upper_inv,
                child_upper_off,
                parent_lower_inv,
                parent_upper_inv,
            )
        ]
    )
    return pl.pallas_call(
        backward_kernel,
        out_shape=(
            jax.ShapeDtypeStruct(child_rhs.shape, BF),
            jax.ShapeDtypeStruct(parent_rhs.shape, BF),
        ),
        in_specs=[smem, vmem, vmem, vmem],
        out_specs=(hbm, hbm),
        scratch_shapes=[mats(), one(), pltpu.SemaphoreType.DMA((2,))],
        compiler_params=pltpu.CompilerParams(vmem_limit_bytes=16 * 2**20),
    )(parent_of, gath, ufwd, mat)


def solution(mesh):
    child = P(("row", "col"), None, None)
    par = P("col", None, None)
    return jax.shard_map(
        on_device,
        mesh=mesh,
        in_specs=(child, par, child, child, child, child, par, par, P(("row", "col"))),
        out_specs=(child, par),
        check_vma=False,
    )
```
